256 devices in a mesh: sec: 64 (over z, y, core), slab: 4 (over x).
Axes of the slice: x: 4, y: 4, z: 8, core: 2. Of those that a mesh axis runs over, the one named last changes fastest.
Arguments:
- basis: bfloat16 [128, 1024, 1024], P('sec'), may hold values from -0.1875 to 0.1875
- fermion: bfloat16 [3, 128, 1024, 1024], P(None, 'sec', None, 'slab'), may hold values from -6 to 6
- partner: int32 [3, 128], P(None, 'sec'), may hold values from 0 to 127, as said below
Outputs:
- rotated: bfloat16 [3, 128, 1024, 1024], P(None, 'sec', 'slab')
The draws below stay inside these ranges and needn't reach their ends.
Inputs may be any that keep to these rules, and one draw needn't show every extreme that they name: partner[f, Q] // 2 equals Q // 2 or (Q // 2 + 1) % 64, so a partner lies in the block of 2 sectors that holds Q or in the next block, the last block's next being the first.
All inputs are finite; a program needn't handle non-finite values.
Results may differ from the reference program's by a relative error of at most 0.0049.
Values may be sent and summed in bfloat16 or wider, within the bound.
A program may use at most 64 MiB of HBM per device.

```python
import jax
import jax.numpy as jnp
from jax import lax

NB = 1024
FL = 3
SEC_DEV = 2
S = 128


def draw_partner(key, part):
    offset = jax.random.randint(key, (FL, S), 1, SEC_DEV + 1)
    sector_ids = jnp.arange(S, dtype=jnp.int32)[None, :]
    target = sector_ids + offset
    result = jnp.where(target < S, target, 2 * S - 1 - target).astype(jnp.int32)
    result = jnp.where(sector_ids == S - 2, S - 1, result)
    result = jnp.where(sector_ids == S - 1, 0, result)
    return result.astype(jnp.int32)


def shard_levels(rng, extent, cuts, smallest, high):
    def one(axis_at, parts):
        heights = jax.random.uniform(jax.random.fold_in(jax.random.fold_in(rng, 6), axis_at), (parts,), jnp.float32, smallest / len(cuts), high / len(cuts))
        return jnp.repeat(jnp.exp(heights), extent[axis_at] // parts).reshape((-1,) + (1,) * (len(extent) - axis_at - 1))

    level = one(*cuts[0])
    for cut in cuts[1:]:
        level = level * one(*cut)
    return level


def normal_values(own_key, dims, deviation, most, pieces=(), kind=jnp.bfloat16):
    drawn = deviation * jax.random.normal(own_key, dims, jnp.float32)
    if pieces:
        drawn = drawn * shard_levels(own_key, dims, pieces, -0.22, 0.18)
    return jnp.clip(drawn, -most, most).astype(kind)


def setup_inputs(seed: int = 0) -> dict:
    key_of = jax.random.split(jax.random.key(seed), 4)
    return {
        "basis": normal_values(key_of[0], (S, NB, NB), NB ** -0.5, 0.1875, ((0, 64),)),
        "fermion": normal_values(key_of[1], (FL, S, NB, NB), 1.0, 6.0, ((1, 64), (3, 4))),
        "partner": draw_partner(jax.random.fold_in(key_of[3], 71), 0),
    }


def reference(basis, fermion, partner):
    def sector(index):
        left_basis = basis[index]
        blocks = []
        for flavour in range(FL):
            half_rotated = jnp.dot(left_basis.T, fermion[flavour, index], preferred_element_type=jnp.float32).astype(jnp.bfloat16)
            right_basis = basis[partner[flavour, index]]
            blocks.append(jnp.dot(half_rotated, right_basis, preferred_element_type=jnp.float32).astype(jnp.bfloat16))
        return jnp.stack(blocks)

    rotated = lax.map(sector, jnp.arange(S, dtype=jnp.int32))
    return jnp.transpose(rotated, (1, 0, 2, 3))
```

```python
import functools

import jax
import jax.numpy as jnp
from jax import lax
from jax.experimental import pallas as pl
from jax.experimental.pallas import tpu as pltpu
from jax.sharding import PartitionSpec as P

MESH = pl.DeviceIdType.MESH
NB = 1024
W = 256
NS = 4
FL = 3
SD = 2
B = FL * SD
SECS = 64
NY = 4
LP = 4


def kernel(
    basis, fermion, partner, out,
    uo, u0, u1, u2, u3, fer, half, hr, rbuf, yb1, yb2,
    lu, lf, lo, d_s, d_r, r1_s, r1_r, r2_s, r2_r, y_s, y_r, l1_s, l1_r, l2_s, l2_r, l3_s, l3_r,
):
    us = (u0, u1, u2, u3)
    sec = lax.axis_index("sec")
    me = lax.axis_index("slab")
    core = lax.rem(sec, 2)
    chip = sec // 2
    y = lax.rem(chip, NY)
    z = chip // NY
    nz = SECS // (2 * NY)
    xp, xm = lax.rem(me + 1, NS), lax.rem(me + 3, NS)
    xo = lax.rem(me + 2, NS)
    right, left = (sec, xp), (sec, xm)
    before = (lax.rem(sec + SECS - 1, SECS), me)
    after = (lax.rem(sec + 1, SECS), me)
    y_up, y_dn = lax.rem(y + 1, NY), lax.rem(y + NY - 1, NY)
    z_first = lax.rem(z + nz - jnp.where(y == 0, 1, 0), nz)
    hop1_to = ((z_first * NY + y_up) * 2, me)
    z_from = lax.rem(z + jnp.where(y == 1, 1, 0), nz)
    hop1_from = ((z_from * NY + y_dn) * 2, me)
    hop2_to = ((z * NY + y_up) * 2, me)
    hop2_from = ((z * NY + y_dn) * 2, me)
    hop3_to = ((z * NY + y_up) * 2 + 1, me)
    hop3_from = ((z * NY + y_dn) * 2, me)
    first_sector = sec * SD

    barrier = pltpu.get_barrier_semaphore()

    def greet(device):
        pl.semaphore_signal(barrier, inc=1, device_id=device, device_id_type=MESH)

    for device in (right, left, before, after):
        greet(device)

    @pl.when(core == 0)
    def _():
        for device in (hop1_to, hop1_from, hop2_to, hop2_from, hop3_to):
            greet(device)

    @pl.when(core == 1)
    def _():
        greet(hop3_from)

    def load_uo(j, q):
        return pltpu.make_async_copy(
            basis.at[q, :, pl.ds(pl.multiple_of(j * W, W), W)], uo.at[j, q], lu.at[j, q]
        )

    def load_f(b, f, q):
        return pltpu.make_async_copy(fermion.at[f, q], fer.at[b], lf.at[b])

    def load_u(j):
        return pltpu.make_async_copy(
            basis.at[:, :, pl.ds(j * W, W)], us[j].at[pl.ds(0, SD)], lo.at[j]
        )

    load_f(0, 0, 0).start()
    for j in (xo, xp, xm, me):
        load_uo(j, 0).start()
    for f in range(1, FL):
        load_f(f, f, 0).start()
    for j in range(NS):
        load_uo(j, 1).start()
    for f in range(FL):
        load_f(FL + f, f, 1).start()
    for j in range(NS):
        load_u(j).start()

    @pl.when(core == 0)
    def _():
        pl.semaphore_wait(barrier, 9)

    @pl.when(core == 1)
    def _():
        pl.semaphore_wait(barrier, 5)

    def follow(j):
        return pltpu.make_async_remote_copy(
            src_ref=uo.at[j], dst_ref=us[j].at[pl.ds(SD, SD)],
            send_sem=y_s.at[j], recv_sem=y_r.at[j], device_id=before, device_id_type=MESH,
        )

    def piece(ref, i):
        return ref.at[i // 2, pl.ds((i % 2) * (NB // 2), NB // 2)]

    def last_piece(i):
        return u3.at[SD + i // 2, pl.ds((i % 2) * (NB // 2), NB // 2)]

    def hop1(i):
        return pltpu.make_async_remote_copy(
            src_ref=piece(uo.at[NS - 1], i), dst_ref=yb1.at[i],
            send_sem=l1_s.at[i], recv_sem=l1_r.at[i], device_id=hop1_to, device_id_type=MESH,
        )

    def hop2(i):
        return pltpu.make_async_remote_copy(
            src_ref=yb1.at[i], dst_ref=yb2.at[i],
            send_sem=l2_s.at[i], recv_sem=l2_r.at[i], device_id=hop2_to, device_id_type=MESH,
        )

    def hop3(i):
        return pltpu.make_async_remote_copy(
            src_ref=yb2.at[i], dst_ref=last_piece(i),
            send_sem=l3_s.at[i], recv_sem=l3_r.at[i], device_id=hop3_to, device_id_type=MESH,
        )

    for q in range(SD):
        for j in range(NS):
            load_uo(j, q).wait()
    for j in range(NS - 1):
        follow(j).start()

    @pl.when(core == 1)
    def _():
        follow(NS - 1).start()

    @pl.when(core == 0)
    def _():
        for i in range(LP):
            hop1(i).start()

    H = W // 2

    def direct(b, k):
        return pltpu.make_async_remote_copy(
            src_ref=half.at[b, (xp, xm)[k]], dst_ref=hr.at[b, me],
            send_sem=d_s.at[b, k], recv_sem=d_r.at[b, k],
            device_id=(right, left)[k], device_id_type=MESH,
        )

    def relay1(b, k):
        return pltpu.make_async_remote_copy(
            src_ref=half.at[b, xo, pl.ds(k * H, H)], dst_ref=rbuf.at[b, k],
            send_sem=r1_s.at[b, k], recv_sem=r1_r.at[b, k],
            device_id=(right, left)[k], device_id_type=MESH,
        )

    def relay2(b, k):
        return pltpu.make_async_remote_copy(
            src_ref=rbuf.at[b, k], dst_ref=hr.at[b, (xm, xp)[k], pl.ds(k * H, H)],
            send_sem=r2_s.at[b, k], recv_sem=r2_r.at[b, k],
            device_id=(right, left)[k], device_id_type=MESH,
        )

    def first_product(b, q, d):
        return lax.dot_general(
            uo[d, q], fer[b], (((0,), (0,)), ((), ())), preferred_element_type=jnp.float32
        ).astype(jnp.bfloat16)

    def stage1(b, _):
        q = b // FL
        load_f(b, 0, 0).wait()
        half[b, xo] = first_product(b, q, xo)
        half[b, xp] = first_product(b, q, xp)
        relay1(b, 0).start()
        relay1(b, 1).start()
        half[b, xm] = first_product(b, q, xm)
        direct(b, 0).start()
        hr[b, me] = first_product(b, q, me)
        direct(b, 1).start()
        return 0

    lax.fori_loop(0, B, stage1, 0)

    def forward_x(b):
        for k in range(2):
            relay1(b, k).wait_recv()
            relay2(b, k).start()

    def forward_y1(i):
        @pl.when(core == 0)
        def _():
            hop1(i).wait_recv()
            hop2(i).start()

    def forward_y2(i):
        @pl.when(core == 0)
        def _():
            hop2(i).wait_recv()
            hop3(i).start()

    forward_y1(0)
    forward_y1(1)
    forward_x(0)
    forward_x(1)
    forward_y1(2)
    forward_y1(3)
    forward_x(2)
    forward_y2(0)
    forward_x(3)
    forward_y2(1)
    forward_y2(2)
    forward_x(4)
    forward_y2(3)
    forward_x(5)

    for j in range(NS):
        load_u(j).wait()

    def second_product(b, f, q, j):
        index = lax.rem(partner[f, q] - first_sector + SECS * SD, 2 * SD)
        rows = jnp.concatenate([hr[b, s] for s in range(NS)], axis=1)
        value = jnp.dot(rows, us[j][index], preferred_element_type=jnp.float32)
        out[f, q, :, j * W:(j + 1) * W] = value.astype(jnp.bfloat16)

    follow(0).wait_recv()
    follow(1).wait_recv()

    def early(b, _):
        for k in range(2):
            direct(b, k).wait_recv()
            relay2(b, k).wait_recv()
        q = b // FL
        f = b - q * FL
        second_product(b, f, q, 0)
        second_product(b, f, q, 1)
        return 0

    lax.fori_loop(0, B, early, 0)
    follow(2).wait_recv()

    @pl.when(core == 0)
    def _():
        follow(3).wait_recv()

    @pl.when(core == 1)
    def _():
        for i in range(LP):
            hop3(i).wait_recv()

    def late(b, _):
        q = b // FL
        f = b - q * FL
        second_product(b, f, q, 2)
        second_product(b, f, q, 3)
        return 0

    lax.fori_loop(0, B, late, 0)

    def drain(b, _):
        for k in range(2):
            direct(b, k).wait_send()
            relay1(b, k).wait_send()
            relay2(b, k).wait_send()
        return 0

    lax.fori_loop(0, B, drain, 0)
    for j in range(NS - 1):
        follow(j).wait_send()

    @pl.when(core == 1)
    def _():
        follow(NS - 1).wait_send()

    @pl.when(core == 0)
    def _():
        for i in range(LP):
            hop1(i).wait_send()
            hop2(i).wait_send()
            hop3(i).wait_send()


def local(basis, fermion, partner):
    bf16 = jnp.bfloat16
    dma = pltpu.SemaphoreType.DMA
    return pl.pallas_call(
        kernel,
        out_shape=jax.ShapeDtypeStruct((FL, SD, W, NB), bf16),
        in_specs=[
            pl.BlockSpec(memory_space=pl.ANY),
            pl.BlockSpec(memory_space=pl.ANY),
            pl.BlockSpec(memory_space=pltpu.SMEM),
        ],
        out_specs=pl.BlockSpec(memory_space=pltpu.VMEM),
        scratch_shapes=[
            pltpu.VMEM((NS, SD, NB, W), bf16),
            *[pltpu.VMEM((2 * SD, NB, W), bf16) for _ in range(NS)],
            pltpu.VMEM((B, NB, W), bf16),
            pltpu.VMEM((B, NS, W, W), bf16),
            pltpu.VMEM((B, NS, W, W), bf16),
            pltpu.VMEM((B, 2, W // 2, W), bf16),
            pltpu.VMEM((LP, NB // 2, W), bf16),
            pltpu.VMEM((LP, NB // 2, W), bf16),
            dma((NS, SD)), dma((B,)), dma((NS,)),
            *[dma((B, 2)) for _ in range(6)],
            dma((NS,)), dma((NS,)),
            *[dma((LP,)) for _ in range(6)],
        ],
        compiler_params=pltpu.CompilerParams(
            collective_id=0, has_side_effects=True, vmem_limit_bytes=60 * 2**20
        ),
    )(basis, fermion, partner)


def solution(mesh):
    placed = (P("sec", None, None), P(None, "sec", None, "slab"), P(None, "sec"))
    return jax.shard_map(
        local, mesh=mesh, in_specs=placed, out_specs=P(None, "sec", "slab", None), check_vma=False
    )
```

```python
import functools

import jax
import jax.numpy as jnp
from jax import lax
from jax.experimental import pallas as pl
from jax.experimental.pallas import tpu as pltpu
from jax.sharding import PartitionSpec as P

MESH = pl.DeviceIdType.MESH
NB = 1024
W = 256
NS = 4
FL = 3
SD = 2
B = FL * SD
SECS = 64
NY = 4
LP = 4
KB = NB // LP
KA = NB - KB


def kernel(
    basis, fermion, partner, out,
    uo, u0, u1, u2a, u2b, u3a, u3b, fer, half, hr, rbuf, yb1, yb2, yb3, acc,
    lu, lf, lo, x_s, x_r, r1_r, y_s, y_r, l1_r, l2_r, l3_r, t_s, t_r,
):
    sec = lax.axis_index("sec")
    me = lax.axis_index("slab")
    core = lax.rem(sec, 2)
    chip = sec // 2
    y = lax.rem(chip, NY)
    z = chip // NY
    nz = SECS // (2 * NY)
    xp, xm = lax.rem(me + 1, NS), lax.rem(me + 3, NS)
    xo = lax.rem(me + 2, NS)
    right, left = (sec, xp), (sec, xm)
    before = (lax.rem(sec + SECS - 1, SECS), me)
    after = (lax.rem(sec + 1, SECS), me)
    y_up, y_dn = lax.rem(y + 1, NY), lax.rem(y + NY - 1, NY)
    hop_to = ((z * NY + y_up) * 2, me)
    hop_from = ((z * NY + y_dn) * 2, me)
    row_dn, row_up = lax.rem(z + nz - 1, nz), lax.rem(z + 1, nz)
    row_to = ((row_dn * NY + y) * 2, me)
    row_from = ((row_up * NY + y) * 2, me)
    end_to = ((z * NY + y_up) * 2 + 1, me)
    end_from = ((z * NY + y_dn) * 2, me)
    turns = y == 2
    first_sector = sec * SD

    barrier = pltpu.get_barrier_semaphore()

    def greet(device):
        pl.semaphore_signal(barrier, inc=1, device_id=device, device_id_type=MESH)

    for device in (right, left, before, after):
        greet(device)

    @pl.when(core == 0)
    def _():
        for device in (hop_to, hop_from, end_to):
            greet(device)

        @pl.when(turns)
        def _():
            greet(row_to)
            greet(row_from)

    @pl.when(core == 1)
    def _():
        greet(end_from)

    def load_uo(j, q):
        return pltpu.make_async_copy(
            basis.at[q, :, pl.ds(pl.multiple_of(j * W, W), W)], uo.at[j, q], lu.at[j, q]
        )

    def load_f(b, f, q):
        return pltpu.make_async_copy(fermion.at[f, q], fer.at[b], lf.at[b])

    def load_u(ref, j, row, rows, n):
        return pltpu.make_async_copy(
            basis.at[:, pl.ds(row, rows), pl.ds(j * W, W)], ref.at[pl.ds(0, SD)], lo.at[n]
        )

    def own_u():
        places = ((u0, 0, 0, NB), (u1, 1, 0, NB), (u2a, 2, 0, KA), (u2b, 2, KA, KB),
                  (u3a, 3, 0, KA), (u3b, 3, KA, KB))
        return [load_u(*place, n) for n, place in enumerate(places)]

    load_f(0, 0, 0).start()
    load_uo(xo, 0).start()
    load_uo(xp, 0).start()

    def follow(src, dst, n):
        return pltpu.make_async_remote_copy(
            src_ref=src, dst_ref=dst.at[pl.ds(SD, SD)],
            send_sem=y_s.at[0], recv_sem=y_r.at[n], device_id=before, device_id_type=MESH,
        )

    follow0 = follow(uo.at[0], u0, 0)
    follow1 = follow(uo.at[1], u1, 1)
    follow2a = follow(uo.at[2, :, pl.ds(0, KA)], u2a, 2)
    follow2b = follow(uo.at[2, :, pl.ds(KA, KB)], u2b, 3)
    follow3a = follow(uo.at[3, :, pl.ds(0, KA)], u3a, 4)
    follow3b = follow(uo.at[3, :, pl.ds(KA, KB)], u3b, 5)

    def hop1(i):
        return pltpu.make_async_remote_copy(
            src_ref=uo.at[3, :, pl.ds(i * KB, KB)], dst_ref=yb1.at[i],
            send_sem=y_s.at[0], recv_sem=l1_r.at[i], device_id=hop_to, device_id_type=MESH,
        )

    def hop2(i):
        return pltpu.make_async_remote_copy(
            src_ref=yb1.at[i], dst_ref=yb2.at[i],
            send_sem=y_s.at[0], recv_sem=l2_r.at[i], device_id=hop_to, device_id_type=MESH,
        )

    def turn(i):
        return pltpu.make_async_remote_copy(
            src_ref=yb2.at[i], dst_ref=yb3.at[i],
            send_sem=t_s.at[0], recv_sem=t_r.at[i], device_id=row_to, device_id_type=MESH,
        )

    def end(i, src):
        if i < LP - 1:
            target = u3a.at[pl.ds(SD, SD), pl.ds(i * KB, KB)]
        else:
            target = u3b.at[pl.ds(SD, SD)]
        return pltpu.make_async_remote_copy(
            src_ref=src.at[i], dst_ref=target,
            send_sem=y_s.at[0], recv_sem=l3_r.at[i], device_id=end_to, device_id_type=MESH,
        )

    H = W // 2

    def direct(b, k):
        return pltpu.make_async_remote_copy(
            src_ref=half.at[b, (xp, xm)[k]], dst_ref=hr.at[b, me],
            send_sem=x_s.at[0], recv_sem=x_r.at[b],
            device_id=(right, left)[k], device_id_type=MESH,
        )

    def relay1(b, k):
        return pltpu.make_async_remote_copy(
            src_ref=half.at[b, xo, pl.ds(k * H, H)], dst_ref=rbuf.at[b, k],
            send_sem=x_s.at[0], recv_sem=r1_r.at[b, k],
            device_id=(right, left)[k], device_id_type=MESH,
        )

    def relay2(b, k):
        return pltpu.make_async_remote_copy(
            src_ref=rbuf.at[b, k], dst_ref=hr.at[b, (xm, xp)[k], pl.ds(k * H, H)],
            send_sem=x_s.at[0], recv_sem=x_r.at[b],
            device_id=(right, left)[k], device_id_type=MESH,
        )

    def first_product(b, q, d):
        return lax.dot_general(
            uo[d, q], fer[b], (((0,), (0,)), ((), ())), preferred_element_type=jnp.float32
        ).astype(jnp.bfloat16)

    load_f(0, 0, 0).wait()
    load_uo(xo, 0).wait()
    for j in (xm, me):
        load_uo(j, 0).start()
    for j in (0, 3, 1, 2):
        load_uo(j, 1).start()
    for f in range(1, FL):
        load_f(f, f, 0).start()
    for f in range(FL):
        load_f(FL + f, f, 1).start()
    half[0, xo] = first_product(0, 0, xo)
    load_uo(xp, 0).wait()
    half[0, xp] = first_product(0, 0, xp)

    @pl.when(core == 1)
    def _():
        pl.semaphore_wait(barrier, 5)

    @pl.when((core == 0) & turns)
    def _():
        pl.semaphore_wait(barrier, 9)

    @pl.when((core == 0) & jnp.logical_not(turns))
    def _():
        pl.semaphore_wait(barrier, 7)

    relay1(0, 0).start()
    relay1(0, 1).start()
    load_uo(xm, 0).wait()
    load_uo(me, 0).wait()
    load_uo(0, 1).wait()

    @pl.when(core == 0)
    def _():
        follow0.start()

    load_uo(3, 1).wait()

    @pl.when(core == 0)
    def _():
        for i in range(LP):
            hop1(i).start()

    half[0, xm] = first_product(0, 0, xm)
    direct(0, 0).start()
    hr[0, me] = first_product(0, 0, me)
    direct(0, 1).start()
    load_uo(1, 1).wait()
    load_uo(2, 1).wait()

    @pl.when(core == 0)
    def _():
        follow1.start()
        follow2a.start()
        follow2b.start()

    def stage1(b, _):
        q = b // FL
        load_f(b, 0, 0).wait()
        half[b, xo] = first_product(b, q, xo)
        half[b, xp] = first_product(b, q, xp)
        relay1(b, 0).start()
        relay1(b, 1).start()
        half[b, xm] = first_product(b, q, xm)
        direct(b, 0).start()
        hr[b, me] = first_product(b, q, me)
        direct(b, 1).start()
        return 0

    lax.fori_loop(1, B, stage1, 0)
    for copy in own_u():
        copy.start()

    @pl.when(core == 1)
    def _():
        for copy in (follow0, follow1, follow2a, follow2b, follow3a, follow3b):
            copy.start()

    def forward_x(b):
        for k in range(2):
            relay1(b, k).wait_recv()
            relay2(b, k).start()

    def forward_y1(i):
        @pl.when(core == 0)
        def _():
            hop1(i).wait_recv()
            hop2(i).start()

    def forward_y2(i):
        @pl.when(core == 0)
        def _():
            hop2(i).wait_recv()

            @pl.when(turns)
            def _():
                turn(i).start()

            @pl.when(jnp.logical_not(turns))
            def _():
                end(i, yb2).start()

    def forward_end(i):
        @pl.when((core == 0) & turns)
        def _():
            turn(i).wait_recv()
            end(i, yb3).start()

    forward_y1(0)
    forward_x(0)
    forward_y1(1)
    forward_x(1)
    forward_y1(2)
    forward_x(2)
    forward_y1(3)
    forward_x(3)
    forward_y2(0)
    forward_y2(1)
    forward_end(0)
    forward_x(4)
    forward_y2(2)
    forward_end(1)
    forward_x(5)
    forward_y2(3)
    forward_end(2)
    forward_end(3)

    for copy in own_u():
        copy.wait()

    def locate(b):
        q = b // FL
        f = b - q * FL
        return f, q, lax.rem(partner[q, f] - first_sector + SECS * SD, 2 * SD)

    def rows_of(b, low, high):
        return jnp.concatenate([hr[b, s] for s in range(low, high)], axis=1)

    def times(rows, ref, index):
        return jnp.dot(rows, ref[index], preferred_element_type=jnp.float32)

    def arrive(b):
        here = hr.at[b, pl.ds(0, NS - 1)]
        pltpu.make_async_copy(here, here, x_r.at[b]).wait()

    def whole(b):
        f, q, index = locate(b)
        rows = rows_of(b, 0, NS)
        out[f, q, :, 0:W] = times(rows, u0, index).astype(jnp.bfloat16)
        out[f, q, :, W:2 * W] = times(rows, u1, index).astype(jnp.bfloat16)

    def part(b):
        f, q, index = locate(b)
        rows = rows_of(b, 0, NS - 1)
        acc[b, 0] = times(rows, u2a, index)
        acc[b, 1] = times(rows, u3a, index)

    def rest(b):
        f, q, index = locate(b)
        rows = hr[b, NS - 1]
        out[f, q, :, 2 * W:3 * W] = (acc[b, 0] + times(rows, u2b, index)).astype(jnp.bfloat16)
        out[f, q, :, 3 * W:4 * W] = (acc[b, 1] + times(rows, u3b, index)).astype(jnp.bfloat16)

    def early(b, _):
        arrive(b)
        whole(b)
        return 0

    def middle(b, _):
        part(b)
        return 0

    def late(b, _):
        arrive(b)
        whole(b)
        part(b)
        return 0

    def last(b, _):
        rest(b)
        return 0

    follow0.wait_recv()
    follow1.wait_recv()
    lax.fori_loop(0, B - 2, early, 0)
    follow2a.wait_recv()

    @pl.when(core == 0)
    def _():
        follow3a.wait_recv()

    @pl.when(core == 1)
    def _():
        for i in range(LP - 1):
            end(i, yb2).wait_recv()

    lax.fori_loop(0, B - 2, middle, 0, unroll=True)
    lax.fori_loop(B - 2, B, late, 0)
    follow2b.wait_recv()

    @pl.when(core == 0)
    def _():
        follow3b.wait_recv()

    @pl.when(core == 1)
    def _():
        end(LP - 1, yb2).wait_recv()

    lax.fori_loop(0, B, last, 0, unroll=True)

    pltpu.make_async_copy(hr, hr, x_s.at[0]).wait()

    @pl.when(core == 0)
    def _():
        pltpu.make_async_copy(fer, fer, y_s.at[0]).wait()
        pltpu.make_async_copy(half, half, y_s.at[0]).wait()

        @pl.when(turns)
        def _():
            pltpu.make_async_copy(yb2, yb2, t_s.at[0]).wait()

    @pl.when(core == 1)
    def _():
        pltpu.make_async_copy(uo, uo, y_s.at[0]).wait()


def write_out(result, out, sems):
    copies = [
        pltpu.make_async_copy(result.at[b // SD, b % SD], out.at[b // SD, b % SD], sems.at[b])
        for b in range(B)
    ]
    for copy in copies:
        copy.start()
    for copy in copies:
        copy.wait()


def local(basis, fermion, partner):
    bf16 = jnp.bfloat16
    dma = pltpu.SemaphoreType.DMA
    result = pl.pallas_call(
        kernel,
        out_shape=pltpu.VMEM((FL, SD, W, NB), bf16),
        in_specs=[
            pl.BlockSpec(memory_space=pltpu.HBM),
            pl.BlockSpec(memory_space=pltpu.HBM),
            pl.BlockSpec(memory_space=pltpu.SMEM),
        ],
        out_specs=pl.BlockSpec(memory_space=pltpu.VMEM),
        scratch_shapes=[
            pltpu.VMEM((NS, SD, NB, W), bf16),
            pltpu.VMEM((2 * SD, NB, W), bf16),
            pltpu.VMEM((2 * SD, NB, W), bf16),
            pltpu.VMEM((2 * SD, KA, W), bf16),
            pltpu.VMEM((2 * SD, KB, W), bf16),
            pltpu.VMEM((2 * SD, KA, W), bf16),
            pltpu.VMEM((2 * SD, KB, W), bf16),
            pltpu.VMEM((B, NB, W), bf16),
            pltpu.VMEM((B, NS, W, W), bf16),
            pltpu.VMEM((B, NS, W, W), bf16),
            pltpu.VMEM((B, 2, W // 2, W), bf16),
            pltpu.VMEM((LP, SD, KB, W), bf16),
            pltpu.VMEM((LP, SD, KB, W), bf16),
            pltpu.VMEM((LP, SD, KB, W), bf16),
            pltpu.VMEM((B, 2, W, W), jnp.float32),
            dma((NS, SD)), dma((B,)), dma((6,)),
            dma((1,)), dma((B,)), dma((B, 2)),
            dma((1,)), dma((6,)), dma((LP,)), dma((LP,)), dma((LP,)), dma((1,)), dma((LP,)),
        ],
        compiler_params=pltpu.CompilerParams(
            collective_id=0, has_side_effects=True, vmem_limit_bytes=56 * 2**20
        ),
    )(basis, fermion, partner.T)
    return pl.pallas_call(
        write_out,
        out_shape=jax.ShapeDtypeStruct((FL, SD, W, NB), bf16),
        in_specs=[pl.BlockSpec(memory_space=pltpu.VMEM)],
        out_specs=pl.BlockSpec(memory_space=pl.ANY),
        scratch_shapes=[dma((B,))],
        compiler_params=pltpu.CompilerParams(vmem_limit_bytes=2**20),
    )(result)


def solution(mesh):
    placed = (P("sec", None, None), P(None, "sec", None, "slab"), P(None, "sec"))
    return jax.shard_map(
        local, mesh=mesh, in_specs=placed, out_specs=P(None, "sec", "slab", None), check_vma=False
    )
```

```python
import functools

import jax
import jax.numpy as jnp
from jax import lax
from jax.experimental import pallas as pl
from jax.experimental.pallas import tpu as pltpu
from jax.sharding import PartitionSpec as P

MESH = pl.DeviceIdType.MESH
NB = 1024
W = 256
NS = 4
FL = 3
SD = 2
B = FL * SD
SECS = 64
NY = 4
LP = 4
KB = NB // LP
KA = NB - KB


def kernel(
    basis, fermion, partner_in, out,
    uo, u0, u1, u2a, u2b, u3a, u3b, fer, half, hr, rbuf, yb1, yb2, yb3, acc,
    lu, lf, lo, x_s, x_r, r1_r, y_s, y_r, l1_r, l2_r, l3_r, t_s, t_r, answer, partner, p_s,
):
    sec = lax.axis_index("sec")
    me = lax.axis_index("slab")
    core = lax.rem(sec, 2)
    chip = sec // 2
    y = lax.rem(chip, NY)
    z = chip // NY
    nz = SECS // (2 * NY)
    xp, xm = lax.rem(me + 1, NS), lax.rem(me + 3, NS)
    xo = lax.rem(me + 2, NS)
    right, left = (sec, xp), (sec, xm)
    before = (lax.rem(sec + SECS - 1, SECS), me)
    after = (lax.rem(sec + 1, SECS), me)
    y_up, y_dn = lax.rem(y + 1, NY), lax.rem(y + NY - 1, NY)
    hop_to = ((z * NY + y_up) * 2, me)
    hop_from = ((z * NY + y_dn) * 2, me)
    row_dn, row_up = lax.rem(z + nz - 1, nz), lax.rem(z + 1, nz)
    row_to = ((row_dn * NY + y) * 2, me)
    row_from = ((row_up * NY + y) * 2, me)
    end_to = ((z * NY + y_up) * 2 + 1, me)
    end_from = ((z * NY + y_dn) * 2, me)
    turns = y == 2
    first_sector = sec * SD

    head = (core == 0) & (y == 0) & (z == 0)
    head_peer = (core == 1) & (y == NY - 1) & (z == nz - 1)
    turn_head = (core == 0) & turns & (z == 0)
    turn_peer = (core == 0) & turns & (z == nz - 1)
    passes = (core == 0) & (y == 1) & (z == 0)
    spare = (core == 0) & (y == 3) & (z == 0)
    spare_to = (core == 1) & (y == 2) & (z == 0)
    barrier = pltpu.get_barrier_semaphore()

    def greet(device):
        pl.semaphore_signal(barrier, inc=1, device_id=device, device_id_type=MESH)

    greet(right)
    greet(left)

    @pl.when(jnp.logical_not(head_peer))
    def _():
        greet(after)

    @pl.when(core == 0)
    def _():
        greet(hop_from)

    @pl.when(core == 1)
    def _():
        greet(end_from)

    @pl.when((core == 0) & turns & (z != nz - 1))
    def _():
        greet(row_from)

    @pl.when(head)
    def _():
        greet(before)

    @pl.when(turn_head)
    def _():
        greet(row_to)

    def load_uo(j, q):
        return pltpu.make_async_copy(
            basis.at[q, :, pl.ds(pl.multiple_of(j * W, W), W)], uo.at[j, q], lu.at[j, q]
        )

    def load_f(b, f, q):
        return pltpu.make_async_copy(fermion.at[f, q], fer.at[b], lf.at[b])

    def load_u(ref, j, row, rows, n):
        return pltpu.make_async_copy(
            basis.at[:, pl.ds(row, rows), pl.ds(j * W, W)], ref.at[pl.ds(0, SD)], lo.at[n]
        )

    def own_u():
        places = ((u0, 0, 0, NB), (u1, 1, 0, NB), (u2a, 2, 0, KA), (u2b, 2, KA, KB),
                  (u3a, 3, 0, KA), (u3b, 3, KA, KB))
        return [load_u(*place, n) for n, place in enumerate(places)]

    load_partner = pltpu.make_async_copy(partner_in, partner, p_s.at[0])
    load_f(0, 0, 0).start()
    load_uo(xo, 0).start()
    load_uo(xp, 0).start()
    load_partner.start()

    def follow(src, dst, n):
        return pltpu.make_async_remote_copy(
            src_ref=src, dst_ref=dst.at[pl.ds(SD, SD)],
            send_sem=y_s.at[0], recv_sem=y_r.at[n], device_id=before, device_id_type=MESH,
        )

    follow0 = follow(basis.at[:, :, pl.ds(0, W)], u0, 0)
    follow1 = follow(basis.at[:, :, pl.ds(W, W)], u1, 1)
    follow2a = follow(basis.at[:, pl.ds(0, KA), pl.ds(2 * W, W)], u2a, 2)
    follow2b = follow(basis.at[:, pl.ds(KA, KB), pl.ds(2 * W, W)], u2b, 3)
    follow3a = follow(basis.at[:, pl.ds(0, KA), pl.ds(3 * W, W)], u3a, 4)
    follow3b = follow(basis.at[:, pl.ds(KA, KB), pl.ds(3 * W, W)], u3b, 5)

    def hop1(i):
        if i < LP:
            source = basis.at[:, pl.ds(i * KB, KB), pl.ds(3 * W, W)]
        else:
            source = basis.at[:, pl.ds(KA, KB), pl.ds(2 * W, W)]
        return pltpu.make_async_remote_copy(
            src_ref=source, dst_ref=yb1.at[i],
            send_sem=y_s.at[0], recv_sem=l1_r.at[i], device_id=hop_to, device_id_type=MESH,
        )

    def hop2(i):
        return pltpu.make_async_remote_copy(
            src_ref=yb1.at[i], dst_ref=yb2.at[i],
            send_sem=y_s.at[0], recv_sem=l2_r.at[i], device_id=hop_to, device_id_type=MESH,
        )

    def turn(i):
        return pltpu.make_async_remote_copy(
            src_ref=yb2.at[i], dst_ref=yb3.at[i],
            send_sem=t_s.at[0], recv_sem=t_r.at[i], device_id=row_to, device_id_type=MESH,
        )

    def end(i, src):
        if i < LP - 1:
            target = u3a.at[pl.ds(SD, SD), pl.ds(i * KB, KB)]
        else:
            target = (u3b if i == LP - 1 else u2b).at[pl.ds(SD, SD)]
        return pltpu.make_async_remote_copy(
            src_ref=src.at[i], dst_ref=target,
            send_sem=y_s.at[0], recv_sem=l3_r.at[i], device_id=end_to, device_id_type=MESH,
        )

    H = W // 2

    def direct(b, k):
        return pltpu.make_async_remote_copy(
            src_ref=half.at[b, (xp, xm)[k]], dst_ref=hr.at[b, me],
            send_sem=x_s.at[0], recv_sem=x_r.at[b],
            device_id=(right, left)[k], device_id_type=MESH,
        )

    def relay1(b, k):
        return pltpu.make_async_remote_copy(
            src_ref=half.at[b, xo, pl.ds(k * H, H)], dst_ref=rbuf.at[b, k],
            send_sem=x_s.at[0], recv_sem=r1_r.at[b, k],
            device_id=(right, left)[k], device_id_type=MESH,
        )

    def relay2(b, k):
        return pltpu.make_async_remote_copy(
            src_ref=rbuf.at[b, k], dst_ref=hr.at[b, (xm, xp)[k], pl.ds(k * H, H)],
            send_sem=x_s.at[0], recv_sem=x_r.at[b],
            device_id=(right, left)[k], device_id_type=MESH,
        )

    def first_product(b, q, d):
        return lax.dot_general(
            uo[d, q], fer[b], (((0,), (0,)), ((), ())), preferred_element_type=jnp.float32
        ).astype(jnp.bfloat16)

    def one(condition):
        return jnp.where(condition, 1, 0)

    greeted = jnp.where(
        core == 1, 3 + one(head_peer), 5 - one(head) + one(turns & (z != 0)) + one(turn_peer)
    )
    pl.semaphore_wait(barrier, greeted)

    @pl.when(turn_peer)
    def _():
        pl.semaphore_signal(answer, inc=1, device_id=row_from, device_id_type=MESH)

    @pl.when(head_peer)
    def _():
        pl.semaphore_signal(answer, inc=1, device_id=after, device_id_type=MESH)

    def send_chunks():
        for copy in (follow0, follow1, follow2a):
            copy.start()

    @pl.when((core == 0) & jnp.logical_not(head))
    def _():
        send_chunks()
        follow2b.start()

    @pl.when(spare)
    def _():
        follow3b.start()

    @pl.when(core == 0)
    def _():
        for i in range(LP - 1):
            hop1(i).start()

    @pl.when((core == 0) & jnp.logical_not(spare))
    def _():
        hop1(LP - 1).start()

    @pl.when(head)
    def _():
        hop1(LP).start()

    load_f(0, 0, 0).wait()
    load_uo(xo, 0).wait()
    for j in (xm, me):
        load_uo(j, 0).start()
    for j in (0, 3, 1, 2):
        load_uo(j, 1).start()
    for f in range(1, FL):
        load_f(f, f, 0).start()
    for f in range(FL):
        load_f(FL + f, f, 1).start()
    for k in range(2):
        half[0, xo, k * H:(k + 1) * H] = lax.dot_general(
            uo[xo, 0, :, k * H:(k + 1) * H], fer[0], (((0,), (0,)), ((), ())),
            preferred_element_type=jnp.float32,
        ).astype(jnp.bfloat16)
    relay1(0, 0).start()
    load_uo(xp, 0).wait()
    half[0, xp] = first_product(0, 0, xp)
    relay1(0, 1).start()
    load_uo(xm, 0).wait()
    half[0, xm] = first_product(0, 0, xm)
    direct(0, 0).start()
    load_uo(me, 0).wait()
    hr[0, me] = first_product(0, 0, me)
    direct(0, 1).start()
    for j in range(NS):
        load_uo(j, 1).wait()

    def stage1(b, _):
        q = b // FL
        load_f(b, 0, 0).wait()
        half[b, xo] = first_product(b, q, xo)
        half[b, xp] = first_product(b, q, xp)
        relay1(b, 0).start()
        relay1(b, 1).start()
        half[b, xm] = first_product(b, q, xm)
        direct(b, 0).start()
        hr[b, me] = first_product(b, q, me)
        direct(b, 1).start()
        return 0

    lax.fori_loop(1, 4, stage1, 0)

    @pl.when(head)
    def _():
        pl.semaphore_wait(answer, 1)
        send_chunks()

    lax.fori_loop(4, B, stage1, 0)
    for copy in own_u():
        copy.start()

    @pl.when(core == 1)
    def _():
        for copy in (follow0, follow1, follow2a, follow2b, follow3a, follow3b):
            copy.start()

    def forward_x(b):
        for k in range(2):
            relay1(b, k).wait_recv()
            relay2(b, k).start()

    def forward_y1(i):
        here = (core == 0, (core == 0) & jnp.logical_not(head), passes)[max(0, i - LP + 2)]

        @pl.when(here)
        def _():
            hop1(i).wait_recv()
            hop2(i).start()

    def forward_y2(i):
        here = (core == 0, (core == 0) & jnp.logical_not(passes), turn_head)[max(0, i - LP + 2)]

        @pl.when(here)
        def _():
            hop2(i).wait_recv()
            if i == 0:
                @pl.when(turn_head)
                def _():
                    pl.semaphore_wait(answer, 1)

            @pl.when(turns)
            def _():
                turn(i).start()

            if i < LP:
                @pl.when(jnp.logical_not(turns))
                def _():
                    end(i, yb2).start()

    def forward_end(i):
        @pl.when((core == 0) & turns if i < LP else turn_peer)
        def _():
            turn(i).wait_recv()
            end(i, yb3).start()

    forward_y1(0)
    forward_x(0)
    forward_y1(1)
    forward_x(1)
    forward_y1(2)
    forward_y1(3)
    forward_x(2)
    forward_y2(0)
    forward_y1(4)
    forward_x(3)
    forward_y2(1)
    forward_end(0)
    forward_y2(2)
    forward_x(4)
    forward_end(1)
    forward_y2(3)
    forward_end(2)
    forward_x(5)
    forward_y2(4)
    forward_end(3)
    forward_end(4)

    load_partner.wait()
    for copy in own_u():
        copy.wait()

    def locate(b):
        q = b // FL
        f = b - q * FL
        return f, q, lax.rem(partner[q, f] - first_sector + SECS * SD, 2 * SD)

    def rows_of(b, low, high):
        return jnp.concatenate([hr[b, s] for s in range(low, high)], axis=1)

    def times(rows, ref, index):
        return jnp.dot(rows, ref[index], preferred_element_type=jnp.float32)

    def arrive(b):
        here = hr.at[b, pl.ds(0, NS - 1)]
        pltpu.make_async_copy(here, here, x_r.at[b]).wait()

    def whole(b):
        f, q, index = locate(b)
        rows = rows_of(b, 0, NS)
        out[f, q, :, 0:W] = times(rows, u0, index).astype(jnp.bfloat16)
        out[f, q, :, W:2 * W] = times(rows, u1, index).astype(jnp.bfloat16)

    def part(b):
        f, q, index = locate(b)
        rows = rows_of(b, 0, NS - 1)
        acc[b, 0] = times(rows, u2a, index)
        acc[b, 1] = times(rows, u3a, index)

    def rest(b):
        f, q, index = locate(b)
        rows = hr[b, NS - 1]
        out[f, q, :, 2 * W:3 * W] = (acc[b, 0] + times(rows, u2b, index)).astype(jnp.bfloat16)
        out[f, q, :, 3 * W:4 * W] = (acc[b, 1] + times(rows, u3b, index)).astype(jnp.bfloat16)

    def early(b, _):
        arrive(b)
        whole(b)
        return 0

    def middle(b, _):
        part(b)
        return 0

    def late(b, _):
        arrive(b)
        whole(b)
        part(b)
        return 0

    def last(b, _):
        rest(b)
        return 0

    follow0.wait_recv()
    follow1.wait_recv()
    lax.fori_loop(0, B - 2, early, 0)
    follow2a.wait_recv()

    @pl.when(core == 0)
    def _():
        follow3a.wait_recv()

    @pl.when(core == 1)
    def _():
        for i in range(LP - 1):
            end(i, yb2).wait_recv()

    lax.fori_loop(0, B - 2, middle, 0, unroll=True)
    lax.fori_loop(B - 2, B, late, 0, unroll=True)

    @pl.when(jnp.logical_not(head_peer))
    def _():
        follow2b.wait_recv()

    @pl.when(head_peer)
    def _():
        end(LP, yb2).wait_recv()

    @pl.when((core == 0) | spare_to)
    def _():
        follow3b.wait_recv()

    @pl.when((core == 1) & jnp.logical_not(spare_to))
    def _():
        end(LP - 1, yb2).wait_recv()

    lax.fori_loop(0, B, last, 0, unroll=True)

    def sent(ref, sem):
        pltpu.make_async_copy(ref, ref, sem.at[0]).wait()

    sent(hr, x_s)

    @pl.when(core == 0)
    def _():
        sent(fer, y_s)
        sent(half.at[pl.ds(0, B - 1)], y_s)

        @pl.when(jnp.logical_not(head))
        def _():
            sent(half.at[0], y_s)

        @pl.when(head | turn_peer)
        def _():
            sent(half.at[0, pl.ds(0, 2)], y_s)

        @pl.when(turns)
        def _():
            sent(yb2.at[pl.ds(0, LP)], t_s)

        @pl.when(turn_head)
        def _():
            sent(yb2.at[LP], t_s)

    @pl.when(core == 1)
    def _():
        sent(uo, y_s)


def local(basis, fermion, partner):
    bf16 = jnp.bfloat16
    dma = pltpu.SemaphoreType.DMA
    result = pl.pallas_call(
        kernel,
        out_shape=pltpu.VMEM((FL, SD, W, NB), bf16),
        in_specs=[
            pl.BlockSpec(memory_space=pltpu.HBM),
            pl.BlockSpec(memory_space=pltpu.HBM),
            pl.BlockSpec(memory_space=pltpu.HBM),
        ],
        out_specs=pl.BlockSpec(memory_space=pltpu.VMEM),
        scratch_shapes=[
            pltpu.VMEM((NS, SD, NB, W), bf16),
            pltpu.VMEM((2 * SD, NB, W), bf16),
            pltpu.VMEM((2 * SD, NB, W), bf16),
            pltpu.VMEM((2 * SD, KA, W), bf16),
            pltpu.VMEM((2 * SD, KB, W), bf16),
            pltpu.VMEM((2 * SD, KA, W), bf16),
            pltpu.VMEM((2 * SD, KB, W), bf16),
            pltpu.VMEM((B, NB, W), bf16),
            pltpu.VMEM((B, NS, W, W), bf16),
            pltpu.VMEM((B, NS, W, W), bf16),
            pltpu.VMEM((B, 2, W // 2, W), bf16),
            pltpu.VMEM((LP + 1, SD, KB, W), bf16),
            pltpu.VMEM((LP + 1, SD, KB, W), bf16),
            pltpu.VMEM((LP + 1, SD, KB, W), bf16),
            pltpu.VMEM((B, 2, W, W), jnp.float32),
            dma((NS, SD)), dma((B,)), dma((6,)),
            dma((1,)), dma((B,)), dma((B, 2)),
            dma((1,)), dma((6,)), *[dma((LP + 1,)) for _ in range(3)], dma((1,)), dma((LP + 1,)), pltpu.SemaphoreType.REGULAR,
            pltpu.SMEM((SD, FL), jnp.int32), dma((1,)),
        ],
        compiler_params=pltpu.CompilerParams(
            collective_id=0, has_side_effects=True, vmem_limit_bytes=56 * 2**20
        ),
    )(basis, fermion, partner.T)
    return result


def solution(mesh):
    placed = (P("sec", None, None), P(None, "sec", None, "slab"), P(None, "sec"))
    return jax.shard_map(
        local, mesh=mesh, in_specs=placed, out_specs=P(None, "sec", "slab", None), check_vma=False
    )
```

```python
import functools

import jax
import jax.numpy as jnp
from jax import lax
from jax.experimental import pallas as pl
from jax.experimental.pallas import tpu as pltpu
from jax.sharding import PartitionSpec as P

MESH = pl.DeviceIdType.MESH
NB = 1024
W = 256
NS = 4
FL = 3
SD = 2
B = FL * SD
SECS = 64
NY = 4
LP = 4
KB = NB // LP
KA = NB - KB
KH = KB // 2


def kernel(
    basis, fermion, partner_in, out,
    uo, u0, u1, u2a, u2b, u3a, u3b, fer, half, hr, rbuf, yb1, yb2, yb3, acc,
    lu, lf, lo, x_s, x_r, r1_r, y_s, y_r, l1_r, l2_r, l3_r, t_s, t_r, answer, partner, p_s,
):
    sec = lax.axis_index("sec")
    me = lax.axis_index("slab")
    core = lax.rem(sec, 2)
    chip = sec // 2
    y = lax.rem(chip, NY)
    z = chip // NY
    nz = SECS // (2 * NY)
    xp, xm = lax.rem(me + 1, NS), lax.rem(me + 3, NS)
    xo = lax.rem(me + 2, NS)
    right, left = (sec, xp), (sec, xm)
    before = (lax.rem(sec + SECS - 1, SECS), me)
    after = (lax.rem(sec + 1, SECS), me)
    y_up, y_dn = lax.rem(y + 1, NY), lax.rem(y + NY - 1, NY)
    hop_to = ((z * NY + y_up) * 2, me)
    hop_from = ((z * NY + y_dn) * 2, me)
    row_dn, row_up = lax.rem(z + nz - 1, nz), lax.rem(z + 1, nz)
    row_to = ((row_dn * NY + y) * 2, me)
    row_from = ((row_up * NY + y) * 2, me)
    end_to = ((z * NY + y_up) * 2 + 1, me)
    end_from = ((z * NY + y_dn) * 2, me)
    turns = y == 2
    first_sector = sec * SD

    head = (core == 0) & (y == 0) & (z == 0)
    head_peer = (core == 1) & (y == NY - 1) & (z == nz - 1)
    turn_head = (core == 0) & turns & (z == 0)
    turn_peer = (core == 0) & turns & (z == nz - 1)
    passes = (core == 0) & (y == 1) & (z == 0)
    spare = (core == 0) & (y == 3) & (z == 0)
    spare_to = (core == 1) & (y == 2) & (z == 0)
    barrier = pltpu.get_barrier_semaphore()

    def greet(device):
        pl.semaphore_signal(barrier, inc=1, device_id=device, device_id_type=MESH)

    greet(right)
    greet(left)

    @pl.when(jnp.logical_not(head_peer))
    def _():
        greet(after)

    @pl.when(core == 0)
    def _():
        greet(hop_from)

    @pl.when(core == 1)
    def _():
        greet(end_from)

    @pl.when((core == 0) & turns & (z != nz - 1))
    def _():
        greet(row_from)

    @pl.when(head)
    def _():
        greet(before)

    @pl.when(turn_head)
    def _():
        greet(row_to)

    def load_uo(j, q):
        return pltpu.make_async_copy(
            basis.at[q, :, pl.ds(pl.multiple_of(j * W, W), W)], uo.at[j, q], lu.at[j if q == 0 else NS]
        )

    def load_f(b, f, q):
        return pltpu.make_async_copy(fermion.at[f, q], fer.at[b], lf.at[b])

    def load_u(ref, j, row, rows):
        return pltpu.make_async_copy(
            basis.at[:, pl.ds(row, rows), pl.ds(j * W, W)], ref.at[pl.ds(0, SD)], lo.at[0]
        )

    def own_u():
        places = ((u0, 0, 0, NB), (u1, 1, 0, NB), (u2a, 2, 0, KA), (u2b, 2, KA, KB),
                  (u3a, 3, 0, KA), (u3b, 3, KA, KB))
        return [load_u(*place) for place in places]

    load_partner = pltpu.make_async_copy(partner_in, partner, p_s.at[0])
    load_f(0, 0, 0).start()
    load_uo(xo, 0).start()
    load_uo(xp, 0).start()
    load_partner.start()

    def follow(src, dst, n):
        return pltpu.make_async_remote_copy(
            src_ref=src, dst_ref=dst.at[pl.ds(SD, SD)],
            send_sem=y_s.at[0], recv_sem=y_r.at[n], device_id=before, device_id_type=MESH,
        )

    follow0 = follow(basis.at[:, :, pl.ds(0, W)], u0, 0)
    follow1 = follow(basis.at[:, :, pl.ds(W, W)], u1, 1)
    follow2a = follow(basis.at[:, pl.ds(0, KA), pl.ds(2 * W, W)], u2a, 2)
    follow2b = follow(basis.at[:, pl.ds(KA, KB), pl.ds(2 * W, W)], u2b, 3)
    follow3a = follow(basis.at[:, pl.ds(0, KA), pl.ds(3 * W, W)], u3a, 4)
    follow3b = follow(basis.at[:, pl.ds(KA, KB), pl.ds(3 * W, W)], u3b, 5)

    follow3c = pltpu.make_async_remote_copy(
        src_ref=basis.at[:, pl.ds(KA + KH, KH), pl.ds(3 * W, W)],
        dst_ref=u3b.at[pl.ds(SD, SD), pl.ds(KH, KH)],
        send_sem=y_s.at[0], recv_sem=y_r.at[5], device_id=before, device_id_type=MESH,
    )

    def hop1(i, rows=KB):
        if i < LP:
            source = basis.at[:, pl.ds(i * KB, rows), pl.ds(3 * W, W)]
        else:
            source = basis.at[:, pl.ds(KA, KB), pl.ds(2 * W, W)]
        return pltpu.make_async_remote_copy(
            src_ref=source, dst_ref=yb1.at[i, :, pl.ds(0, rows)],
            send_sem=y_s.at[0], recv_sem=l1_r.at[i], device_id=hop_to, device_id_type=MESH,
        )

    def hop2(i, rows=KB):
        return pltpu.make_async_remote_copy(
            src_ref=yb1.at[i, :, pl.ds(0, rows)], dst_ref=yb2.at[i, :, pl.ds(0, rows)],
            send_sem=y_s.at[0], recv_sem=l2_r.at[i], device_id=hop_to, device_id_type=MESH,
        )

    def turn(i):
        return pltpu.make_async_remote_copy(
            src_ref=yb2.at[i], dst_ref=yb3.at[i],
            send_sem=t_s.at[0], recv_sem=t_r.at[i], device_id=row_to, device_id_type=MESH,
        )

    def end(i, src, rows=KB):
        if i < LP - 1:
            target = u3a.at[pl.ds(SD, SD), pl.ds(i * KB, KB)]
        else:
            target = (u3b if i == LP - 1 else u2b).at[pl.ds(SD, SD), pl.ds(0, rows)]
        return pltpu.make_async_remote_copy(
            src_ref=src.at[i, :, pl.ds(0, rows)], dst_ref=target,
            send_sem=y_s.at[0], recv_sem=l3_r.at[max(0, i - LP + 2)], device_id=end_to, device_id_type=MESH,
        )

    H = W // 2

    def direct(b, k):
        return pltpu.make_async_remote_copy(
            src_ref=half.at[b, (xp, xm)[k]], dst_ref=hr.at[b, me],
            send_sem=x_s.at[0], recv_sem=x_r.at[b],
            device_id=(right, left)[k], device_id_type=MESH,
        )

    def relay1(b, k):
        return pltpu.make_async_remote_copy(
            src_ref=half.at[b, xo, pl.ds(k * H, H)], dst_ref=rbuf.at[b, k],
            send_sem=x_s.at[0], recv_sem=r1_r.at[b],
            device_id=(right, left)[k], device_id_type=MESH,
        )

    def relay2(b, k):
        return pltpu.make_async_remote_copy(
            src_ref=rbuf.at[b, k], dst_ref=hr.at[b, (xm, xp)[k], pl.ds(k * H, H)],
            send_sem=x_s.at[0], recv_sem=x_r.at[b],
            device_id=(right, left)[k], device_id_type=MESH,
        )

    def first_product(b, q, d):
        return lax.dot_general(
            uo[d, q], fer[b], (((0,), (0,)), ((), ())), preferred_element_type=jnp.float32
        ).astype(jnp.bfloat16)

    def one(condition):
        return jnp.where(condition, 1, 0)

    greeted = jnp.where(
        core == 1, 3 + one(head_peer), 5 - one(head) + one(turns & (z != 0)) + one(turn_peer)
    )
    pl.semaphore_wait(barrier, greeted)

    @pl.when(turn_peer)
    def _():
        pl.semaphore_signal(answer, inc=1, device_id=row_from, device_id_type=MESH)

    @pl.when(head_peer)
    def _():
        pl.semaphore_signal(answer, inc=1, device_id=after, device_id_type=MESH)

    def send_chunks():
        for copy in (follow0, follow1, follow2a):
            copy.start()

    @pl.when((core == 0) & jnp.logical_not(head))
    def _():
        send_chunks()
        follow2b.start()

    @pl.when(spare)
    def _():
        follow3c.start()

    @pl.when(core == 0)
    def _():
        for i in range(LP - 1):
            hop1(i).start()

    @pl.when((core == 0) & jnp.logical_not(spare))
    def _():
        hop1(LP - 1).start()

    @pl.when(spare)
    def _():
        hop1(LP - 1, KH).start()

    @pl.when(head)
    def _():
        hop1(LP).start()

    load_f(0, 0, 0).wait()
    load_uo(xo, 0).wait()
    for j in (xm, me):
        load_uo(j, 0).start()
    for j in (0, 3, 1, 2):
        load_uo(j, 1).start()
    for f in range(1, FL):
        load_f(f, f, 0).start()
    for f in range(FL):
        load_f(FL + f, f, 1).start()
    for k in range(2):
        half[0, xo, k * H:(k + 1) * H] = lax.dot_general(
            uo[xo, 0, :, k * H:(k + 1) * H], fer[0], (((0,), (0,)), ((), ())),
            preferred_element_type=jnp.float32,
        ).astype(jnp.bfloat16)
    relay1(0, 0).start()
    load_uo(xp, 0).wait()
    half[0, xp] = first_product(0, 0, xp)
    relay1(0, 1).start()
    load_uo(xm, 0).wait()
    half[0, xm] = first_product(0, 0, xm)
    direct(0, 0).start()
    load_uo(me, 0).wait()
    hr[0, me] = first_product(0, 0, me)
    direct(0, 1).start()
    second = uo.at[:, 1]
    pltpu.make_async_copy(second, second, lu.at[NS]).wait()

    def stage1(b, _):
        q = b // FL
        load_f(b, 0, 0).wait()
        half[b, xo] = first_product(b, q, xo)
        half[b, xp] = first_product(b, q, xp)
        relay1(b, 0).start()
        relay1(b, 1).start()
        half[b, xm] = first_product(b, q, xm)
        direct(b, 0).start()
        hr[b, me] = first_product(b, q, me)
        direct(b, 1).start()
        return 0

    lax.fori_loop(1, 4, stage1, 0)

    @pl.when(head)
    def _():
        pl.semaphore_wait(answer, 1)
        send_chunks()

    lax.fori_loop(4, B, stage1, 0)
    for copy in own_u():
        copy.start()

    @pl.when(core == 1)
    def _():
        for copy in (follow0, follow1, follow2a, follow2b, follow3a, follow3b):
            copy.start()

    def forward_x(b):
        pltpu.make_async_copy(rbuf.at[b], rbuf.at[b], r1_r.at[b]).wait()
        for k in range(2):
            relay2(b, k).start()

    def forward_y1(i):
        short = (i == LP - 1) & head
        if i < LP:
            @pl.when((core == 0) & jnp.logical_not(short))
            def _():
                hop1(i).wait_recv()
                hop2(i).start()

        if i >= LP - 1:
            rows = KH if i == LP - 1 else KB

            @pl.when(short if i == LP - 1 else passes)
            def _():
                hop1(i, rows).wait_recv()
                hop2(i, rows).start()

    def forward_y2(i):
        short = (i == LP - 1) & passes
        if i < LP:
            @pl.when((core == 0) & jnp.logical_not(turns | short))
            def _():
                hop2(i).wait_recv()
                end(i, yb2).start()

        @pl.when((core == 0) & turns if i < LP else turn_head)
        def _():
            hop2(i).wait_recv()
            if i == 0:
                @pl.when(turn_head)
                def _():
                    pl.semaphore_wait(answer, 1)

            turn(i).start()

        if i == LP - 1:
            @pl.when(passes)
            def _():
                hop2(i, KH).wait_recv()
                end(i, yb2, KH).start()

    def forward_end(i):
        @pl.when((core == 0) & turns if i < LP else turn_peer)
        def _():
            turn(i).wait_recv()
            end(i, yb3).start()

    forward_y1(0)
    forward_x(0)
    forward_y1(1)
    forward_x(1)
    forward_y1(2)
    forward_y1(3)
    forward_x(2)
    forward_y2(0)
    forward_y1(4)
    forward_x(3)
    forward_y2(1)
    forward_end(0)
    forward_y2(2)
    forward_x(4)
    forward_end(1)
    forward_y2(3)
    forward_end(2)
    forward_x(5)
    forward_y2(4)
    forward_end(3)
    forward_end(4)

    load_partner.wait()
    pltpu.make_async_copy(uo, uo, lo.at[0]).wait()

    def locate(b):
        q = b // FL
        f = b - q * FL
        return f, q, lax.rem(partner[q, f] - first_sector + SECS * SD, 2 * SD)

    def rows_of(b, low, high):
        return jnp.concatenate([hr[b, s] for s in range(low, high)], axis=1)

    def times(rows, ref, index):
        return jnp.dot(rows, ref[index], preferred_element_type=jnp.float32)

    def arrive(b):
        here = hr.at[b, pl.ds(0, NS - 1)]
        pltpu.make_async_copy(here, here, x_r.at[b]).wait()

    def whole(b):
        f, q, index = locate(b)
        rows = rows_of(b, 0, NS)
        out[f, q, :, 0:W] = times(rows, u0, index).astype(jnp.bfloat16)
        out[f, q, :, W:2 * W] = times(rows, u1, index).astype(jnp.bfloat16)

    def part(b):
        f, q, index = locate(b)
        rows = rows_of(b, 0, NS - 1)
        acc[b, 0] = times(rows, u2a, index)
        acc[b, 1] = times(rows, u3a, index)

    def rest(b, j):
        f, q, index = locate(b)
        value = acc[b, j] + times(hr[b, NS - 1], (u2b, u3b)[j], index)
        out[f, q, :, (2 + j) * W:(3 + j) * W] = value.astype(jnp.bfloat16)

    def early(b, _):
        arrive(b)
        whole(b)
        return 0

    def middle(b, _):
        part(b)
        return 0

    def late(b, _):
        arrive(b)
        whole(b)
        part(b)
        return 0

    def last(j):
        def body(b, _):
            rest(b, j)
            return 0

        lax.fori_loop(0, B, body, 0, unroll=True)

    follow0.wait_recv()
    follow1.wait_recv()
    lax.fori_loop(0, B - 2, early, 0)

    @pl.when(head_peer)
    def _():
        lax.fori_loop(B - 2, B, early, 0)

    follow2a.wait_recv()

    @pl.when(core == 0)
    def _():
        follow3a.wait_recv()

    @pl.when(core == 1)
    def _():
        pieces = u3a.at[pl.ds(SD, SD)]
        pltpu.make_async_copy(pieces, pieces, l3_r.at[0]).wait()

    lax.fori_loop(0, B - 2, middle, 0, unroll=True)

    @pl.when(head_peer)
    def _():
        lax.fori_loop(B - 2, B, middle, 0, unroll=True)

    @pl.when(jnp.logical_not(head_peer))
    def _():
        lax.fori_loop(B - 2, B, late, 0, unroll=True)
        follow2b.wait_recv()
        last(0)

    @pl.when(core == 0)
    def _():
        follow3b.wait_recv()

    @pl.when((core == 1) & jnp.logical_not(spare_to))
    def _():
        end(LP - 1, yb2).wait_recv()

    @pl.when(spare_to)
    def _():
        end(LP - 1, yb2, KH).wait_recv()
        follow3c.wait_recv()

    last(1)

    @pl.when(head_peer)
    def _():
        end(LP, yb2).wait_recv()
        last(0)

    def sent(ref, sem):
        pltpu.make_async_copy(ref, ref, sem.at[0]).wait()

    sent(hr, x_s)

    @pl.when(core == 0)
    def _():
        sent(fer, y_s)
        sent(half.at[pl.ds(0, B - 1)], y_s)

        @pl.when(jnp.logical_not(head))
        def _():
            sent(half.at[0], y_s)

        @pl.when(head)
        def _():
            sent(half.at[0, pl.ds(0, 3)], y_s)

        @pl.when(passes)
        def _():
            sent(half.at[0, 0], y_s)

        @pl.when(turn_peer)
        def _():
            sent(half.at[0, pl.ds(0, 2)], y_s)

        @pl.when(turns)
        def _():
            sent(yb2.at[pl.ds(0, LP)], t_s)

        @pl.when(turn_head)
        def _():
            sent(yb2.at[LP], t_s)

    @pl.when(core == 1)
    def _():
        sent(uo, y_s)


def local(basis, fermion, partner):
    bf16 = jnp.bfloat16
    dma = pltpu.SemaphoreType.DMA
    result = pl.pallas_call(
        kernel,
        out_shape=pltpu.VMEM((FL, SD, W, NB), bf16),
        in_specs=[
            pl.BlockSpec(memory_space=pltpu.HBM),
            pl.BlockSpec(memory_space=pltpu.HBM),
            pl.BlockSpec(memory_space=pltpu.HBM),
        ],
        out_specs=pl.BlockSpec(memory_space=pltpu.VMEM),
        scratch_shapes=[
            pltpu.VMEM((NS, SD, NB, W), bf16),
            pltpu.VMEM((2 * SD, NB, W), bf16),
            pltpu.VMEM((2 * SD, NB, W), bf16),
            pltpu.VMEM((2 * SD, KA, W), bf16),
            pltpu.VMEM((2 * SD, KB, W), bf16),
            pltpu.VMEM((2 * SD, KA, W), bf16),
            pltpu.VMEM((2 * SD, KB, W), bf16),
            pltpu.VMEM((B, NB, W), bf16),
            pltpu.VMEM((B, NS, W, W), bf16),
            pltpu.VMEM((B, NS, W, W), bf16),
            pltpu.VMEM((B, 2, W // 2, W), bf16),
            pltpu.VMEM((LP + 1, SD, KB, W), bf16),
            pltpu.VMEM((LP + 1, SD, KB, W), bf16),
            pltpu.VMEM((LP + 1, SD, KB, W), bf16),
            pltpu.VMEM((B, 2, W, W), jnp.float32),
            dma((NS + 1,)), dma((B,)), dma((1,)),
            dma((1,)), dma((B,)), dma((B,)),
            dma((1,)), dma((6,)), dma((LP + 1,)), dma((LP + 1,)), dma((3,)), dma((1,)), dma((LP + 1,)), pltpu.SemaphoreType.REGULAR,
            pltpu.SMEM((SD, FL), jnp.int32), dma((1,)),
        ],
        compiler_params=pltpu.CompilerParams(
            collective_id=0, has_side_effects=True, vmem_limit_bytes=56 * 2**20
        ),
    )(basis, fermion, partner.T)
    return result


def solution(mesh):
    placed = (P("sec", None, None), P(None, "sec", None, "slab"), P(None, "sec"))
    return jax.shard_map(
        local, mesh=mesh, in_specs=placed, out_specs=P(None, "sec", "slab", None), check_vma=False
    )
```

```python
import functools

import jax
import jax.numpy as jnp
from jax import lax
from jax.experimental import pallas as pl
from jax.experimental.pallas import tpu as pltpu
from jax.sharding import PartitionSpec as P

MESH = pl.DeviceIdType.MESH
NB = 1024
W = 256
NS = 4
FL = 3
SD = 2
B = FL * SD
SECS = 64
NY = 4
LP = 4
KB = NB // LP
KA = NB - KB
KH = KB // 2


def kernel(
    basis, fermion, partner_in, out,
    uo, u0, u1, u2a, u2b, u3a, u3b, fer, half, hr, rbuf, yb1, yb2, yb3, acc,
    lu, lf, lo, x_s, x_r, r1_r, y_s, y_r, l1_r, l2_r, l3_r, t_s, t_r, answer, x_answer, partner, p_s,
):
    sec = lax.axis_index("sec")
    me = lax.axis_index("slab")
    core = lax.rem(sec, 2)
    chip = sec // 2
    y = lax.rem(chip, NY)
    z = chip // NY
    nz = SECS // (2 * NY)
    xp, xm = lax.rem(me + 1, NS), lax.rem(me + 3, NS)
    xo = lax.rem(me + 2, NS)
    right, left = (sec, xp), (sec, xm)
    before = (lax.rem(sec + SECS - 1, SECS), me)
    after = (lax.rem(sec + 1, SECS), me)
    y_up, y_dn = lax.rem(y + 1, NY), lax.rem(y + NY - 1, NY)
    hop_to = ((z * NY + y_up) * 2, me)
    hop_from = ((z * NY + y_dn) * 2, me)
    row_dn, row_up = lax.rem(z + nz - 1, nz), lax.rem(z + 1, nz)
    row_to = ((row_dn * NY + y) * 2, me)
    row_from = ((row_up * NY + y) * 2, me)
    end_to = ((z * NY + y_up) * 2 + 1, me)
    end_from = ((z * NY + y_dn) * 2, me)
    turns = y == 2
    first_sector = sec * SD

    head = (core == 0) & (y == 0) & (z == 0)
    head_peer = (core == 1) & (y == NY - 1) & (z == nz - 1)
    turn_head = (core == 0) & turns & (z == 0)
    turn_peer = (core == 0) & turns & (z == nz - 1)
    passes = (core == 0) & (y == 1) & (z == 0)
    spare = (core == 0) & (y == 3) & (z == 0)
    spare_to = (core == 1) & (y == 2) & (z == 0)
    barrier = pltpu.get_barrier_semaphore()

    def greet(device):
        pl.semaphore_signal(barrier, inc=1, device_id=device, device_id_type=MESH)

    @pl.when(me != NS - 1)
    def _():
        greet(right)

    @pl.when(me != 1)
    def _():
        greet(left)

    @pl.when(jnp.logical_not(head_peer))
    def _():
        greet(after)

    @pl.when(core == 0)
    def _():
        greet(hop_from)

    @pl.when(core == 1)
    def _():
        greet(end_from)

    @pl.when((core == 0) & turns & (z != nz - 1))
    def _():
        greet(row_from)

    @pl.when(head)
    def _():
        greet(before)

    @pl.when(turn_head)
    def _():
        greet(row_to)

    def load_uo(j, q):
        return pltpu.make_async_copy(
            basis.at[q, :, pl.ds(pl.multiple_of(j * W, W), W)], uo.at[j, q], lu.at[j if q == 0 else NS]
        )

    def load_f(b, f, q):
        return pltpu.make_async_copy(fermion.at[f, q], fer.at[b], lf.at[b])

    def load_u(ref, j, row, rows):
        return pltpu.make_async_copy(
            basis.at[:, pl.ds(row, rows), pl.ds(j * W, W)], ref.at[pl.ds(0, SD)], lo.at[0]
        )

    def own_u():
        places = ((u0, 0, 0, NB), (u1, 1, 0, NB), (u2a, 2, 0, KA), (u2b, 2, KA, KB),
                  (u3a, 3, 0, KA), (u3b, 3, KA, KB))
        return [load_u(*place) for place in places]

    load_partner = pltpu.make_async_copy(partner_in, partner, p_s.at[0])
    load_f(0, 0, 0).start()
    load_uo(xo, 0).start()
    load_uo(xp, 0).start()
    load_partner.start()

    def follow(src, dst, n):
        return pltpu.make_async_remote_copy(
            src_ref=src, dst_ref=dst.at[pl.ds(SD, SD)],
            send_sem=y_s.at[0], recv_sem=y_r.at[n], device_id=before, device_id_type=MESH,
        )

    follow0 = follow(basis.at[:, :, pl.ds(0, W)], u0, 0)
    follow1 = follow(basis.at[:, :, pl.ds(W, W)], u1, 1)
    follow2a = follow(basis.at[:, pl.ds(0, KA), pl.ds(2 * W, W)], u2a, 2)
    follow2b = follow(basis.at[:, pl.ds(KA, KB), pl.ds(2 * W, W)], u2b, 3)
    follow3a = follow(basis.at[:, pl.ds(0, KA), pl.ds(3 * W, W)], u3a, 4)
    follow3b = follow(basis.at[:, pl.ds(KA, KB), pl.ds(3 * W, W)], u3b, 5)

    follow3c = pltpu.make_async_remote_copy(
        src_ref=basis.at[:, pl.ds(KA + KH, KH), pl.ds(3 * W, W)],
        dst_ref=u3b.at[pl.ds(SD, SD), pl.ds(KH, KH)],
        send_sem=y_s.at[0], recv_sem=y_r.at[5], device_id=before, device_id_type=MESH,
    )

    def hop1(i, rows=KB):
        if i < LP:
            source = basis.at[:, pl.ds(i * KB, rows), pl.ds(3 * W, W)]
        else:
            source = basis.at[:, pl.ds(KA, KB), pl.ds(2 * W, W)]
        return pltpu.make_async_remote_copy(
            src_ref=source, dst_ref=yb1.at[i, :, pl.ds(0, rows)],
            send_sem=y_s.at[0], recv_sem=l1_r.at[i], device_id=hop_to, device_id_type=MESH,
        )

    def hop2(i, rows=KB):
        return pltpu.make_async_remote_copy(
            src_ref=yb1.at[i, :, pl.ds(0, rows)], dst_ref=yb2.at[i, :, pl.ds(0, rows)],
            send_sem=y_s.at[0], recv_sem=l2_r.at[i], device_id=hop_to, device_id_type=MESH,
        )

    def turn(i):
        return pltpu.make_async_remote_copy(
            src_ref=yb2.at[i], dst_ref=yb3.at[i],
            send_sem=t_s.at[0], recv_sem=t_r.at[i], device_id=row_to, device_id_type=MESH,
        )

    def end(i, src, rows=KB):
        if i < LP - 1:
            target = u3a.at[pl.ds(SD, SD), pl.ds(i * KB, KB)]
        else:
            target = (u3b if i == LP - 1 else u2b).at[pl.ds(SD, SD), pl.ds(0, rows)]
        return pltpu.make_async_remote_copy(
            src_ref=src.at[i, :, pl.ds(0, rows)], dst_ref=target,
            send_sem=y_s.at[0], recv_sem=l3_r.at[max(0, i - LP + 2)], device_id=end_to, device_id_type=MESH,
        )

    H = W // 2

    def direct(b, k):
        return pltpu.make_async_remote_copy(
            src_ref=half.at[b, (xp, xm)[k]], dst_ref=hr.at[b, me],
            send_sem=x_s.at[0], recv_sem=x_r.at[b],
            device_id=(right, left)[k], device_id_type=MESH,
        )

    def relay1(b, k):
        return pltpu.make_async_remote_copy(
            src_ref=half.at[b, xo, pl.ds(k * H, H)], dst_ref=rbuf.at[b, k],
            send_sem=x_s.at[0], recv_sem=r1_r.at[b],
            device_id=(right, left)[k], device_id_type=MESH,
        )

    def relay2(b, k):
        return pltpu.make_async_remote_copy(
            src_ref=rbuf.at[b, k], dst_ref=hr.at[b, (xm, xp)[k], pl.ds(k * H, H)],
            send_sem=x_s.at[0], recv_sem=x_r.at[b],
            device_id=(right, left)[k], device_id_type=MESH,
        )

    def first_product(b, q, d):
        return lax.dot_general(
            uo[d, q], fer[b], (((0,), (0,)), ((), ())), preferred_element_type=jnp.float32
        ).astype(jnp.bfloat16)

    def one(condition):
        return jnp.where(condition, 1, 0)

    greeted = jnp.where(
        core == 1, 3 + one(head_peer), 5 - one(head) + one(turns & (z != 0)) + one(turn_peer)
    )
    pl.semaphore_wait(barrier, greeted - 2 * one(me == 0))

    @pl.when(me == 1)
    def _():
        pl.semaphore_signal(x_answer, inc=1, device_id=left, device_id_type=MESH)

    @pl.when(me == NS - 1)
    def _():
        pl.semaphore_signal(x_answer, inc=1, device_id=right, device_id_type=MESH)

    @pl.when(turn_peer)
    def _():
        pl.semaphore_signal(answer, inc=1, device_id=row_from, device_id_type=MESH)

    @pl.when(head_peer)
    def _():
        pl.semaphore_signal(answer, inc=1, device_id=after, device_id_type=MESH)

    def send_chunks():
        for copy in (follow0, follow1, follow2a):
            copy.start()

    @pl.when((core == 0) & jnp.logical_not(head))
    def _():
        send_chunks()
        follow2b.start()

    @pl.when(spare)
    def _():
        follow3c.start()

    @pl.when(core == 0)
    def _():
        for i in range(LP - 1):
            hop1(i).start()

    @pl.when((core == 0) & jnp.logical_not(spare))
    def _():
        hop1(LP - 1).start()

    @pl.when(spare)
    def _():
        hop1(LP - 1, KH).start()

    @pl.when(head)
    def _():
        hop1(LP).start()

    load_f(0, 0, 0).wait()
    load_uo(xo, 0).wait()
    for j in (xm, me):
        load_uo(j, 0).start()
    for j in (0, 3, 1, 2):
        load_uo(j, 1).start()
    for f in range(1, FL):
        load_f(f, f, 0).start()
    for f in range(FL):
        load_f(FL + f, f, 1).start()
    for k in range(2):
        half[0, xo, k * H:(k + 1) * H] = lax.dot_general(
            uo[xo, 0, :, k * H:(k + 1) * H], fer[0], (((0,), (0,)), ((), ())),
            preferred_element_type=jnp.float32,
        ).astype(jnp.bfloat16)

    @pl.when(me == 0)
    def _():
        pl.semaphore_wait(x_answer, 2)

    relay1(0, 0).start()
    load_uo(xp, 0).wait()
    half[0, xp] = first_product(0, 0, xp)
    relay1(0, 1).start()
    load_uo(xm, 0).wait()
    half[0, xm] = first_product(0, 0, xm)
    direct(0, 0).start()
    load_uo(me, 0).wait()
    hr[0, me] = first_product(0, 0, me)
    direct(0, 1).start()
    second = uo.at[:, 1]
    pltpu.make_async_copy(second, second, lu.at[NS]).wait()

    def stage1(b, _):
        q = b // FL
        load_f(b, 0, 0).wait()
        half[b, xo] = first_product(b, q, xo)
        half[b, xp] = first_product(b, q, xp)
        relay1(b, 0).start()
        relay1(b, 1).start()
        half[b, xm] = first_product(b, q, xm)
        direct(b, 0).start()
        hr[b, me] = first_product(b, q, me)
        direct(b, 1).start()
        return 0

    lax.fori_loop(1, 4, stage1, 0)

    @pl.when(head)
    def _():
        pl.semaphore_wait(answer, 1)
        send_chunks()

    lax.fori_loop(4, B, stage1, 0)
    for copy in own_u():
        copy.start()

    @pl.when(core == 1)
    def _():
        for copy in (follow0, follow1, follow2a, follow2b, follow3a, follow3b):
            copy.start()

    def forward_x(b):
        pltpu.make_async_copy(rbuf.at[b], rbuf.at[b], r1_r.at[b]).wait()
        for k in range(2):
            relay2(b, k).start()

    def forward_y1(i):
        short = (i == LP - 1) & head
        if i < LP:
            @pl.when((core == 0) & jnp.logical_not(short))
            def _():
                hop1(i).wait_recv()
                hop2(i).start()

        if i >= LP - 1:
            rows = KH if i == LP - 1 else KB

            @pl.when(short if i == LP - 1 else passes)
            def _():
                hop1(i, rows).wait_recv()
                hop2(i, rows).start()

    def forward_y2(i):
        short = (i == LP - 1) & passes
        if i < LP:
            @pl.when((core == 0) & jnp.logical_not(turns | short))
            def _():
                hop2(i).wait_recv()
                end(i, yb2).start()

        @pl.when((core == 0) & turns if i < LP else turn_head)
        def _():
            hop2(i).wait_recv()
            if i == 0:
                @pl.when(turn_head)
                def _():
                    pl.semaphore_wait(answer, 1)

            turn(i).start()

        if i == LP - 1:
            @pl.when(passes)
            def _():
                hop2(i, KH).wait_recv()
                end(i, yb2, KH).start()

    def forward_end(i):
        @pl.when((core == 0) & turns if i < LP else turn_peer)
        def _():
            turn(i).wait_recv()
            end(i, yb3).start()

    forward_y1(0)
    forward_x(0)
    forward_y1(1)
    forward_x(1)
    forward_y1(2)
    forward_y1(3)
    forward_x(2)
    forward_y2(0)
    forward_y1(4)
    forward_x(3)
    forward_y2(1)
    forward_end(0)
    forward_y2(2)
    forward_x(4)
    forward_end(1)
    forward_y2(3)
    forward_end(2)
    forward_x(5)
    forward_y2(4)
    forward_end(3)
    forward_end(4)

    load_partner.wait()
    pltpu.make_async_copy(uo, uo, lo.at[0]).wait()

    def locate(b):
        q = b // FL
        f = b - q * FL
        return f, q, lax.rem(partner[q, f] - first_sector + SECS * SD, 2 * SD)

    def rows_of(b, low, high):
        return jnp.concatenate([hr[b, s] for s in range(low, high)], axis=1)

    def times(rows, ref, index):
        return jnp.dot(rows, ref[index], preferred_element_type=jnp.float32)

    def arrive(b):
        here = hr.at[b, pl.ds(0, NS - 1)]
        pltpu.make_async_copy(here, here, x_r.at[b]).wait()

    def whole(b):
        f, q, index = locate(b)
        rows = rows_of(b, 0, NS)
        out[f, q, :, 0:W] = times(rows, u0, index).astype(jnp.bfloat16)
        out[f, q, :, W:2 * W] = times(rows, u1, index).astype(jnp.bfloat16)

    def part(b, j):
        f, q, index = locate(b)
        acc[b, j] = times(rows_of(b, 0, NS - 1), (u2a, u3a)[j], index)

    def rest(b, j):
        f, q, index = locate(b)
        value = acc[b, j] + times(hr[b, NS - 1], (u2b, u3b)[j], index)
        out[f, q, :, (2 + j) * W:(3 + j) * W] = value.astype(jnp.bfloat16)

    def early(b, _):
        arrive(b)
        whole(b)
        return 0

    def middle(b, _):
        part(b, 0)
        part(b, 1)
        return 0

    def late(b, _):
        arrive(b)
        whole(b)
        part(b, 0)
        part(b, 1)
        return 0

    def parts(j):
        def body(b, _):
            part(b, j)
            return 0

        lax.fori_loop(0, B, body, 0, unroll=True)

    def last(j):
        def body(b, _):
            rest(b, j)
            return 0

        lax.fori_loop(0, B, body, 0, unroll=True)

    follow0.wait_recv()
    follow1.wait_recv()
    lax.fori_loop(0, B - 2, early, 0)

    @pl.when(core == 0)
    def _():
        follow3a.wait_recv()

    def long_way():
        pieces = u3a.at[pl.ds(SD, SD)]
        pltpu.make_async_copy(pieces, pieces, l3_r.at[0]).wait()

    @pl.when(head_peer)
    def _():
        lax.fori_loop(B - 2, B, early, 0)
        long_way()
        parts(1)
        follow2a.wait_recv()
        parts(0)

    @pl.when(jnp.logical_not(head_peer))
    def _():
        follow2a.wait_recv()

        @pl.when(core == 1)
        def _():
            long_way()

        lax.fori_loop(0, B - 2, middle, 0, unroll=True)
        lax.fori_loop(B - 2, B, late, 0, unroll=True)
        follow2b.wait_recv()
        last(0)

    @pl.when(core == 0)
    def _():
        follow3b.wait_recv()

    @pl.when((core == 1) & jnp.logical_not(spare_to))
    def _():
        end(LP - 1, yb2).wait_recv()

    @pl.when(spare_to)
    def _():
        end(LP - 1, yb2, KH).wait_recv()
        follow3c.wait_recv()

    last(1)

    @pl.when(head_peer)
    def _():
        end(LP, yb2).wait_recv()
        last(0)

    def sent(ref, sem):
        pltpu.make_async_copy(ref, ref, sem.at[0]).wait()

    sent(hr, x_s)

    @pl.when(core == 0)
    def _():
        sent(fer, y_s)
        sent(half.at[pl.ds(0, B - 1)], y_s)

        @pl.when(jnp.logical_not(head))
        def _():
            sent(half.at[0], y_s)

        @pl.when(head)
        def _():
            sent(half.at[0, pl.ds(0, 3)], y_s)

        @pl.when(passes)
        def _():
            sent(half.at[0, 0], y_s)

        @pl.when(turn_peer)
        def _():
            sent(half.at[0, pl.ds(0, 2)], y_s)

        @pl.when(turns)
        def _():
            sent(yb2.at[pl.ds(0, LP)], t_s)

        @pl.when(turn_head)
        def _():
            sent(yb2.at[LP], t_s)

    @pl.when(core == 1)
    def _():
        sent(uo, y_s)


def local(basis, fermion, partner):
    bf16 = jnp.bfloat16
    dma = pltpu.SemaphoreType.DMA
    result = pl.pallas_call(
        kernel,
        out_shape=pltpu.VMEM((FL, SD, W, NB), bf16),
        in_specs=[
            pl.BlockSpec(memory_space=pltpu.HBM),
            pl.BlockSpec(memory_space=pltpu.HBM),
            pl.BlockSpec(memory_space=pltpu.HBM),
        ],
        out_specs=pl.BlockSpec(memory_space=pltpu.VMEM),
        scratch_shapes=[
            pltpu.VMEM((NS, SD, NB, W), bf16),
            pltpu.VMEM((2 * SD, NB, W), bf16),
            pltpu.VMEM((2 * SD, NB, W), bf16),
            pltpu.VMEM((2 * SD, KA, W), bf16),
            pltpu.VMEM((2 * SD, KB, W), bf16),
            pltpu.VMEM((2 * SD, KA, W), bf16),
            pltpu.VMEM((2 * SD, KB, W), bf16),
            pltpu.VMEM((B, NB, W), bf16),
            pltpu.VMEM((B, NS, W, W), bf16),
            pltpu.VMEM((B, NS, W, W), bf16),
            pltpu.VMEM((B, 2, W // 2, W), bf16),
            pltpu.VMEM((LP + 1, SD, KB, W), bf16),
            pltpu.VMEM((LP + 1, SD, KB, W), bf16),
            pltpu.VMEM((LP + 1, SD, KB, W), bf16),
            pltpu.VMEM((B, 2, W, W), jnp.float32),
            dma((NS + 1,)), dma((B,)), dma((1,)),
            dma((1,)), dma((B,)), dma((B,)),
            dma((1,)), dma((6,)), dma((LP + 1,)), dma((LP + 1,)), dma((3,)), dma((1,)), dma((LP + 1,)), pltpu.SemaphoreType.REGULAR, pltpu.SemaphoreType.REGULAR,
            pltpu.SMEM((SD, FL), jnp.int32), dma((1,)),
        ],
        compiler_params=pltpu.CompilerParams(
            collective_id=0, has_side_effects=True, vmem_limit_bytes=56 * 2**20
        ),
    )(basis, fermion, partner.T)
    return result


def solution(mesh):
    placed = (P("sec", None, None), P(None, "sec", None, "slab"), P(None, "sec"))
    return jax.shard_map(
        local, mesh=mesh, in_specs=placed, out_specs=P(None, "sec", "slab", None), check_vma=False
    )
```

```python
import functools

import jax
import jax.numpy as jnp
from jax import lax
from jax.experimental import pallas as pl
from jax.experimental.pallas import tpu as pltpu
from jax.sharding import PartitionSpec as P

MESH = pl.DeviceIdType.MESH
NB = 1024
W = 256
NS = 4
FL = 3
SD = 2
B = FL * SD
SECS = 64
NY = 4
LP = 4
KB = NB // LP
KA = NB - KB
KH = KB // 2


def kernel(
    basis, fermion, partner_in, out,
    uo, u0, u1, u2a, u2b, u3a, u3b, fer, half, hr, rbuf, yb1, yb2, yb3, acc,
    lu, lf, lo, x_s, x_r, r1_r, y_s, y_r, l1_r, l2_r, l3_r, t_s, t_r, answer, x_answer, partner, p_s,
):
    sec = lax.axis_index("sec")
    me = lax.axis_index("slab")
    core = lax.rem(sec, 2)
    chip = sec // 2
    y = lax.rem(chip, NY)
    z = chip // NY
    nz = SECS // (2 * NY)
    xp, xm = lax.rem(me + 1, NS), lax.rem(me + 3, NS)
    xo = lax.rem(me + 2, NS)
    right, left = (sec, xp), (sec, xm)
    before = (lax.rem(sec + SECS - 1, SECS), me)
    after = (lax.rem(sec + 1, SECS), me)
    y_up, y_dn = lax.rem(y + 1, NY), lax.rem(y + NY - 1, NY)
    hop_to = ((z * NY + y_up) * 2, me)
    hop_from = ((z * NY + y_dn) * 2, me)
    row_dn, row_up = lax.rem(z + nz - 1, nz), lax.rem(z + 1, nz)
    row_to = ((row_dn * NY + y) * 2, me)
    row_from = ((row_up * NY + y) * 2, me)
    end_to = ((z * NY + y_up) * 2 + 1, me)
    end_from = ((z * NY + y_dn) * 2, me)
    turns = y == 2
    first_sector = sec * SD

    head = (core == 0) & (y == 0) & (z == 0)
    head_peer = (core == 1) & (y == NY - 1) & (z == nz - 1)
    turn_head = (core == 0) & turns & (z == 0)
    turn_peer = (core == 0) & turns & (z == nz - 1)
    passes = (core == 0) & (y == 1) & (z == 0)
    spare = (core == 0) & (y == 3) & (z == 0)
    spare_to = (core == 1) & (y == 2) & (z == 0)
    barrier = pltpu.get_barrier_semaphore()

    def greet(device):
        pl.semaphore_signal(barrier, inc=1, device_id=device, device_id_type=MESH)

    @pl.when(me != NS - 1)
    def _():
        greet(right)

    @pl.when(me != 1)
    def _():
        greet(left)

    @pl.when(jnp.logical_not(head_peer))
    def _():
        greet(after)

    @pl.when(core == 0)
    def _():
        greet(hop_from)

    @pl.when(core == 1)
    def _():
        greet(end_from)

    @pl.when((core == 0) & turns & (z != nz - 1))
    def _():
        greet(row_from)

    @pl.when(head)
    def _():
        greet(before)

    @pl.when(turn_head)
    def _():
        greet(row_to)

    def load_uo(j, q):
        return pltpu.make_async_copy(
            basis.at[q, :, pl.ds(pl.multiple_of(j * W, W), W)], uo.at[j, q], lu.at[j if q == 0 else NS]
        )

    def load_f(b, f, q):
        return pltpu.make_async_copy(fermion.at[f, q], fer.at[b], lf.at[b])

    def load_u(ref, j, row, rows):
        return pltpu.make_async_copy(
            basis.at[:, pl.ds(row, rows), pl.ds(j * W, W)], ref.at[pl.ds(0, SD)], lo.at[0]
        )

    def own_u():
        places = ((u0, 0, 0, NB), (u1, 1, 0, NB), (u2a, 2, 0, KA), (u2b, 2, KA, KB),
                  (u3a, 3, 0, KA), (u3b, 3, KA, KB))
        return [load_u(*place) for place in places]

    load_partner = pltpu.make_async_copy(partner_in, partner, p_s.at[0])
    load_f(0, 0, 0).start()
    load_uo(xo, 0).start()
    load_uo(xp, 0).start()
    load_partner.start()

    def follow(src, dst, n):
        return pltpu.make_async_remote_copy(
            src_ref=src, dst_ref=dst.at[pl.ds(SD, SD)],
            send_sem=y_s.at[0], recv_sem=y_r.at[n], device_id=before, device_id_type=MESH,
        )

    follow0 = follow(basis.at[:, :, pl.ds(0, W)], u0, 0)
    follow1 = follow(basis.at[:, :, pl.ds(W, W)], u1, 1)
    follow2a = follow(basis.at[:, pl.ds(0, KA), pl.ds(2 * W, W)], u2a, 2)
    follow2b = follow(basis.at[:, pl.ds(KA, KB), pl.ds(2 * W, W)], u2b, 3)
    follow3a = follow(basis.at[:, pl.ds(0, KA), pl.ds(3 * W, W)], u3a, 4)
    follow3b = follow(basis.at[:, pl.ds(KA, KB), pl.ds(3 * W, W)], u3b, 5)

    follow3c = pltpu.make_async_remote_copy(
        src_ref=basis.at[:, pl.ds(KA + KH, KH), pl.ds(3 * W, W)],
        dst_ref=u3b.at[pl.ds(SD, SD), pl.ds(KH, KH)],
        send_sem=y_s.at[0], recv_sem=y_r.at[5], device_id=before, device_id_type=MESH,
    )

    def hop1(i, rows=KB):
        if i < LP:
            source = basis.at[:, pl.ds(i * KB, rows), pl.ds(3 * W, W)]
        else:
            source = basis.at[:, pl.ds(KA, KB), pl.ds(2 * W, W)]
        return pltpu.make_async_remote_copy(
            src_ref=source, dst_ref=yb1.at[i, :, pl.ds(0, rows)],
            send_sem=y_s.at[0], recv_sem=l1_r.at[i], device_id=hop_to, device_id_type=MESH,
        )

    def hop2(i, rows=KB):
        return pltpu.make_async_remote_copy(
            src_ref=yb1.at[i, :, pl.ds(0, rows)], dst_ref=yb2.at[i, :, pl.ds(0, rows)],
            send_sem=y_s.at[0], recv_sem=l2_r.at[i], device_id=hop_to, device_id_type=MESH,
        )

    def turn(i):
        return pltpu.make_async_remote_copy(
            src_ref=yb2.at[i], dst_ref=yb3.at[i],
            send_sem=t_s.at[0], recv_sem=t_r.at[i], device_id=row_to, device_id_type=MESH,
        )

    def end(i, src, rows=KB):
        if i < LP - 1:
            target = u3a.at[pl.ds(SD, SD), pl.ds(i * KB, KB)]
        else:
            target = (u3b if i == LP - 1 else u2b).at[pl.ds(SD, SD), pl.ds(0, rows)]
        return pltpu.make_async_remote_copy(
            src_ref=src.at[i, :, pl.ds(0, rows)], dst_ref=target,
            send_sem=y_s.at[0], recv_sem=l3_r.at[max(0, i - LP + 2)], device_id=end_to, device_id_type=MESH,
        )

    H = W // 2

    def direct(b, k):
        return pltpu.make_async_remote_copy(
            src_ref=half.at[b, (xp, xm)[k]], dst_ref=hr.at[b, me],
            send_sem=x_s.at[0], recv_sem=x_r.at[b],
            device_id=(right, left)[k], device_id_type=MESH,
        )

    def relay1(b, k):
        return pltpu.make_async_remote_copy(
            src_ref=half.at[b, xo, pl.ds(k * H, H)], dst_ref=rbuf.at[b, k],
            send_sem=x_s.at[0], recv_sem=r1_r.at[b],
            device_id=(right, left)[k], device_id_type=MESH,
        )

    def relay2(b, k):
        return pltpu.make_async_remote_copy(
            src_ref=rbuf.at[b, k], dst_ref=hr.at[b, (xm, xp)[k], pl.ds(k * H, H)],
            send_sem=x_s.at[0], recv_sem=x_r.at[b],
            device_id=(right, left)[k], device_id_type=MESH,
        )

    def first_product(b, q, d):
        return lax.dot_general(
            uo[d, q], fer[b], (((0,), (0,)), ((), ())), preferred_element_type=jnp.float32
        ).astype(jnp.bfloat16)

    def one(condition):
        return jnp.where(condition, 1, 0)

    greeted = jnp.where(
        core == 1, 3 + one(head_peer), 5 - one(head) + one(turns & (z != 0)) + one(turn_peer)
    )
    pl.semaphore_wait(barrier, greeted - 2 * one(me == 0))

    @pl.when(me == 1)
    def _():
        pl.semaphore_signal(x_answer, inc=1, device_id=left, device_id_type=MESH)

    @pl.when(me == NS - 1)
    def _():
        pl.semaphore_signal(x_answer, inc=1, device_id=right, device_id_type=MESH)

    @pl.when(turn_peer)
    def _():
        pl.semaphore_signal(answer, inc=1, device_id=row_from, device_id_type=MESH)

    @pl.when(head_peer)
    def _():
        pl.semaphore_signal(answer, inc=1, device_id=after, device_id_type=MESH)

    def send_chunks():
        for copy in (follow0, follow1, follow2a):
            copy.start()

    @pl.when((core == 0) & jnp.logical_not(head))
    def _():
        send_chunks()
        follow2b.start()

    @pl.when(spare)
    def _():
        follow3c.start()

    @pl.when(core == 0)
    def _():
        for i in range(LP - 1):
            hop1(i).start()

    @pl.when((core == 0) & jnp.logical_not(spare))
    def _():
        hop1(LP - 1).start()

    @pl.when(spare)
    def _():
        hop1(LP - 1, KH).start()

    @pl.when(head)
    def _():
        hop1(LP).start()

    load_f(0, 0, 0).wait()
    load_uo(xo, 0).wait()
    for j in (xm, me):
        load_uo(j, 0).start()
    for k in range(2):
        half[0, xo, k * H:(k + 1) * H] = lax.dot_general(
            uo[xo, 0, :, k * H:(k + 1) * H], fer[0], (((0,), (0,)), ((), ())),
            preferred_element_type=jnp.float32,
        ).astype(jnp.bfloat16)

    @pl.when(me == 0)
    def _():
        pl.semaphore_wait(x_answer, 2)

    relay1(0, 0).start()
    for f in range(1, FL):
        load_f(f, f, 0).start()
    for j in range(NS):
        load_uo(j, 1).start()
    for f in range(FL):
        load_f(FL + f, f, 1).start()
    load_uo(xp, 0).wait()
    half[0, xp] = first_product(0, 0, xp)
    relay1(0, 1).start()
    load_uo(xm, 0).wait()
    half[0, xm] = first_product(0, 0, xm)
    direct(0, 0).start()
    load_uo(me, 0).wait()
    hr[0, me] = first_product(0, 0, me)
    direct(0, 1).start()
    second = uo.at[:, 1]
    pltpu.make_async_copy(second, second, lu.at[NS]).wait()

    def stage1(b, _):
        q = b // FL
        load_f(b, 0, 0).wait()
        half[b, xo] = first_product(b, q, xo)
        half[b, xp] = first_product(b, q, xp)
        relay1(b, 0).start()
        relay1(b, 1).start()
        half[b, xm] = first_product(b, q, xm)
        direct(b, 0).start()
        hr[b, me] = first_product(b, q, me)
        direct(b, 1).start()
        return 0

    lax.fori_loop(1, 2, stage1, 0)

    @pl.when(head)
    def _():
        pl.semaphore_wait(answer, 1)
        send_chunks()

    lax.fori_loop(2, B, stage1, 0)
    for copy in own_u():
        copy.start()

    @pl.when(core == 1)
    def _():
        for copy in (follow0, follow1, follow2a, follow2b, follow3a, follow3b):
            copy.start()

    def forward_x(b):
        pltpu.make_async_copy(rbuf.at[b], rbuf.at[b], r1_r.at[b]).wait()
        for k in range(2):
            relay2(b, k).start()

    def forward_y1(i):
        short = (i == LP - 1) & head
        if i < LP:
            @pl.when((core == 0) & jnp.logical_not(short))
            def _():
                hop1(i).wait_recv()
                hop2(i).start()

        if i >= LP - 1:
            rows = KH if i == LP - 1 else KB

            @pl.when(short if i == LP - 1 else passes)
            def _():
                hop1(i, rows).wait_recv()
                hop2(i, rows).start()

    def forward_y2(i):
        short = (i == LP - 1) & passes
        if i < LP:
            @pl.when((core == 0) & jnp.logical_not(turns | short))
            def _():
                hop2(i).wait_recv()
                end(i, yb2).start()

        @pl.when((core == 0) & turns if i < LP else turn_head)
        def _():
            hop2(i).wait_recv()
            if i == 0:
                @pl.when(turn_head)
                def _():
                    pl.semaphore_wait(answer, 1)

            turn(i).start()

        if i == LP - 1:
            @pl.when(passes)
            def _():
                hop2(i, KH).wait_recv()
                end(i, yb2, KH).start()

    def forward_end(i):
        @pl.when((core == 0) & turns if i < LP else turn_peer)
        def _():
            turn(i).wait_recv()
            end(i, yb3).start()

    forward_y1(0)
    forward_x(0)
    forward_y1(1)
    forward_x(1)
    forward_y1(2)
    forward_y1(3)
    forward_x(2)
    forward_y2(0)
    forward_y1(4)
    forward_x(3)
    forward_y2(1)
    forward_end(0)
    forward_y2(2)
    forward_x(4)
    forward_end(1)
    forward_y2(3)
    forward_end(2)
    forward_x(5)
    forward_y2(4)
    forward_end(3)
    forward_end(4)

    load_partner.wait()
    pltpu.make_async_copy(uo, uo, lo.at[0]).wait()

    def locate(b):
        q = b // FL
        f = b - q * FL
        return f, q, lax.rem(partner[q, f] - first_sector + SECS * SD, 2 * SD)

    def rows_of(b, low, high):
        return jnp.concatenate([hr[b, s] for s in range(low, high)], axis=1)

    def times(rows, ref, index):
        return jnp.dot(rows, ref[index], preferred_element_type=jnp.float32)

    def arrive(b):
        here = hr.at[b, pl.ds(0, NS - 1)]
        pltpu.make_async_copy(here, here, x_r.at[b]).wait()

    def whole(b):
        f, q, index = locate(b)
        rows = rows_of(b, 0, NS)
        out[f, q, :, 0:W] = times(rows, u0, index).astype(jnp.bfloat16)
        out[f, q, :, W:2 * W] = times(rows, u1, index).astype(jnp.bfloat16)

    def part(b, j):
        f, q, index = locate(b)
        acc[b, j] = times(rows_of(b, 0, NS - 1), (u2a, u3a)[j], index)

    def rest(b, j):
        f, q, index = locate(b)
        value = acc[b, j] + times(hr[b, NS - 1], (u2b, u3b)[j], index)
        out[f, q, :, (2 + j) * W:(3 + j) * W] = value.astype(jnp.bfloat16)

    def early(b, _):
        arrive(b)
        whole(b)
        return 0

    def late(b, _):
        arrive(b)
        whole(b)
        part(b, 0)
        part(b, 1)
        return 0

    def complete(b, _):
        arrive(b)
        whole(b)
        f, q, index = locate(b)
        most, rows = rows_of(b, 0, NS - 1), hr[b, NS - 1]
        for j, (ua, ub) in enumerate(((u2a, u2b), (u3a, u3b))):
            value = times(most, ua, index) + times(rows, ub, index)
            out[f, q, :, (2 + j) * W:(3 + j) * W] = value.astype(jnp.bfloat16)
        return 0

    def parts(j, low, high):
        def body(b, _):
            part(b, j)
            return 0

        lax.fori_loop(low, high, body, 0, unroll=True)

    def last(j):
        def body(b, _):
            rest(b, j)
            return 0

        lax.fori_loop(0, B, body, 0, unroll=True)

    def long_way():
        pieces = u3a.at[pl.ds(SD, SD)]
        pltpu.make_async_copy(pieces, pieces, l3_r.at[0]).wait()

    @pl.when(core == 0)
    def _():
        for copy in (follow0, follow1, follow2a, follow2b, follow3a, follow3b):
            copy.wait_recv()
        lax.fori_loop(0, B, complete, 0)

    late_direct = head_peer | ((core == 1) & (y == NY - 1) & (z == nz // 2 - 1))

    @pl.when(core == 1)
    def _():
        follow0.wait_recv()
        follow1.wait_recv()
        lax.fori_loop(0, B - 2, early, 0)

        @pl.when(late_direct)
        def _():
            early(B - 2, 0)
            long_way()
            parts(1, 0, B - 1)
            follow2a.wait_recv()
            parts(0, 0, B - 1)
            late(B - 1, 0)

        @pl.when(jnp.logical_not(late_direct))
        def _():
            follow2a.wait_recv()
            parts(0, 0, B - 2)
            early(B - 2, 0)
            part(B - 2, 0)
            long_way()
            parts(1, 0, B - 1)
            late(B - 1, 0)
            follow2b.wait_recv()
            last(0)

        @pl.when(jnp.logical_not(spare_to))
        def _():
            end(LP - 1, yb2).wait_recv()

        @pl.when(spare_to)
        def _():
            end(LP - 1, yb2, KH).wait_recv()
            follow3c.wait_recv()

        last(1)

        @pl.when(late_direct)
        def _():
            @pl.when(head_peer)
            def _():
                end(LP, yb2).wait_recv()

            @pl.when(jnp.logical_not(head_peer))
            def _():
                follow2b.wait_recv()

            last(0)

    def sent(ref, sem):
        pltpu.make_async_copy(ref, ref, sem.at[0]).wait()

    sent(hr, x_s)

    @pl.when(core == 0)
    def _():
        sent(fer, y_s)
        sent(half.at[pl.ds(0, B - 1)], y_s)

        @pl.when(jnp.logical_not(head))
        def _():
            sent(half.at[0], y_s)

        @pl.when(head)
        def _():
            sent(half.at[0, pl.ds(0, 3)], y_s)

        @pl.when(passes)
        def _():
            sent(half.at[0, 0], y_s)

        @pl.when(turn_peer)
        def _():
            sent(half.at[0, pl.ds(0, 2)], y_s)

        @pl.when(turns)
        def _():
            sent(yb2.at[pl.ds(0, LP)], t_s)

        @pl.when(turn_head)
        def _():
            sent(yb2.at[LP], t_s)

    @pl.when(core == 1)
    def _():
        sent(uo, y_s)


def local(basis, fermion, partner):
    bf16 = jnp.bfloat16
    dma = pltpu.SemaphoreType.DMA
    result = pl.pallas_call(
        kernel,
        out_shape=pltpu.VMEM((FL, SD, W, NB), bf16),
        in_specs=[
            pl.BlockSpec(memory_space=pltpu.HBM),
            pl.BlockSpec(memory_space=pltpu.HBM),
            pl.BlockSpec(memory_space=pltpu.HBM),
        ],
        out_specs=pl.BlockSpec(memory_space=pltpu.VMEM),
        scratch_shapes=[
            pltpu.VMEM((NS, SD, NB, W), bf16),
            pltpu.VMEM((2 * SD, NB, W), bf16),
            pltpu.VMEM((2 * SD, NB, W), bf16),
            pltpu.VMEM((2 * SD, KA, W), bf16),
            pltpu.VMEM((2 * SD, KB, W), bf16),
            pltpu.VMEM((2 * SD, KA, W), bf16),
            pltpu.VMEM((2 * SD, KB, W), bf16),
            pltpu.VMEM((B, NB, W), bf16),
            pltpu.VMEM((B, NS, W, W), bf16),
            pltpu.VMEM((B, NS, W, W), bf16),
            pltpu.VMEM((B, 2, W // 2, W), bf16),
            pltpu.VMEM((LP + 1, SD, KB, W), bf16),
            pltpu.VMEM((LP + 1, SD, KB, W), bf16),
            pltpu.VMEM((LP + 1, SD, KB, W), bf16),
            pltpu.VMEM((B, 2, W, W), jnp.float32),
            dma((NS + 1,)), dma((B,)), dma((1,)),
            dma((1,)), dma((B,)), dma((B,)),
            dma((1,)), dma((6,)), dma((LP + 1,)), dma((LP + 1,)), dma((3,)), dma((1,)), dma((LP + 1,)), pltpu.SemaphoreType.REGULAR, pltpu.SemaphoreType.REGULAR,
            pltpu.SMEM((SD, FL), jnp.int32), dma((1,)),
        ],
        compiler_params=pltpu.CompilerParams(
            collective_id=0, has_side_effects=True, vmem_limit_bytes=56 * 2**20
        ),
    )(basis, fermion, partner.T)
    return result


def solution(mesh):
    placed = (P("sec", None, None), P(None, "sec", None, "slab"), P(None, "sec"))
    return jax.shard_map(
        local, mesh=mesh, in_specs=placed, out_specs=P(None, "sec", "slab", None), check_vma=False
    )
```

```python
import functools

import jax
import jax.numpy as jnp
from jax import lax
from jax.experimental import pallas as pl
from jax.experimental.pallas import tpu as pltpu
from jax.sharding import PartitionSpec as P

MESH = pl.DeviceIdType.MESH
NB = 1024
W = 256
NS = 4
FL = 3
SD = 2
B = FL * SD
SECS = 64
NY = 4
LP = 4
KB = NB // LP
KA = NB - KB
KH = KB // 2


def kernel(
    basis, fermion, partner_in, out,
    uo, u0, u1, u2a, u2b, u3a, u3b, fer, half, hr, rbuf, yb1, yb2, yb3, acc,
    lu, lf, lo, x_s, x_r, r1_r, y_s, y_r, l1_r, l2_r, l3_r, t_s, t_r, answer, x_answer, partner, p_s,
):
    sec = lax.axis_index("sec")
    me = lax.axis_index("slab")
    core = lax.rem(sec, 2)
    chip = sec // 2
    y = lax.rem(chip, NY)
    z = chip // NY
    nz = SECS // (2 * NY)
    xp, xm = lax.rem(me + 1, NS), lax.rem(me + 3, NS)
    xo = lax.rem(me + 2, NS)
    right, left = (sec, xp), (sec, xm)
    before = (lax.rem(sec + SECS - 1, SECS), me)
    after = (lax.rem(sec + 1, SECS), me)
    y_up, y_dn = lax.rem(y + 1, NY), lax.rem(y + NY - 1, NY)
    hop_to = ((z * NY + y_up) * 2, me)
    hop_from = ((z * NY + y_dn) * 2, me)
    row_dn, row_up = lax.rem(z + nz - 1, nz), lax.rem(z + 1, nz)
    row_to = ((row_dn * NY + y) * 2, me)
    row_from = ((row_up * NY + y) * 2, me)
    end_to = ((z * NY + y_up) * 2 + 1, me)
    end_from = ((z * NY + y_dn) * 2, me)
    turns = y == 2
    first_sector = sec * SD

    head = (core == 0) & (y == 0) & (z == 0)
    head_peer = (core == 1) & (y == NY - 1) & (z == nz - 1)
    turn_head = (core == 0) & turns & (z == 0)
    turn_peer = (core == 0) & turns & (z == nz - 1)
    passes = (core == 0) & (y == 1) & (z == 0)
    spare = (core == 0) & (y == 3) & (z == 0)
    spare_to = (core == 1) & (y == 2) & (z == 0)
    barrier = pltpu.get_barrier_semaphore()

    def greet(device):
        pl.semaphore_signal(barrier, inc=1, device_id=device, device_id_type=MESH)

    @pl.when(me < NS // 2)
    def _():
        greet(right)

    @pl.when((me == 0) | (me == NS - 1))
    def _():
        greet(left)

    @pl.when(jnp.logical_not(head_peer))
    def _():
        greet(after)

    @pl.when(core == 0)
    def _():
        greet(hop_from)

    @pl.when(core == 1)
    def _():
        greet(end_from)

    @pl.when((core == 0) & turns & (z != nz - 1))
    def _():
        greet(row_from)

    @pl.when(head)
    def _():
        greet(before)

    @pl.when(turn_head)
    def _():
        greet(row_to)

    def load_uo(j, q):
        return pltpu.make_async_copy(
            basis.at[q, :, pl.ds(pl.multiple_of(j * W, W), W)], uo.at[j, q], lu.at[j if q == 0 else NS]
        )

    def load_f(b, f, q):
        return pltpu.make_async_copy(fermion.at[f, q], fer.at[b], lf.at[b])

    def load_u(ref, j, row, rows):
        return pltpu.make_async_copy(
            basis.at[:, pl.ds(row, rows), pl.ds(j * W, W)], ref.at[pl.ds(0, SD)], lo.at[0]
        )

    def own_u():
        places = ((u0, 0, 0, NB), (u1, 1, 0, NB), (u2a, 2, 0, KA), (u2b, 2, KA, KB),
                  (u3a, 3, 0, KA), (u3b, 3, KA, KB))
        return [load_u(*place) for place in places]

    load_partner = pltpu.make_async_copy(partner_in, partner, p_s.at[0])
    load_f(0, 0, 0).start()
    load_uo(xo, 0).start()
    load_uo(xp, 0).start()
    load_partner.start()

    def follow(src, dst, n):
        return pltpu.make_async_remote_copy(
            src_ref=src, dst_ref=dst.at[pl.ds(SD, SD)],
            send_sem=y_s.at[0], recv_sem=y_r.at[n], device_id=before, device_id_type=MESH,
        )

    follow0 = follow(basis.at[:, :, pl.ds(0, W)], u0, 0)
    follow1 = follow(basis.at[:, :, pl.ds(W, W)], u1, 1)
    follow2a = follow(basis.at[:, pl.ds(0, KA), pl.ds(2 * W, W)], u2a, 2)
    follow2b = follow(basis.at[:, pl.ds(KA, KB), pl.ds(2 * W, W)], u2b, 3)
    follow3a = follow(basis.at[:, pl.ds(0, KA), pl.ds(3 * W, W)], u3a, 4)
    follow3b = follow(basis.at[:, pl.ds(KA, KB), pl.ds(3 * W, W)], u3b, 5)

    follow3c = pltpu.make_async_remote_copy(
        src_ref=basis.at[:, pl.ds(KA + KH, KH), pl.ds(3 * W, W)],
        dst_ref=u3b.at[pl.ds(SD, SD), pl.ds(KH, KH)],
        send_sem=y_s.at[0], recv_sem=y_r.at[5], device_id=before, device_id_type=MESH,
    )

    def hop1(i, rows=KB):
        if i < LP:
            source = basis.at[:, pl.ds(i * KB, rows), pl.ds(3 * W, W)]
        else:
            source = basis.at[:, pl.ds(KA, KB), pl.ds(2 * W, W)]
        return pltpu.make_async_remote_copy(
            src_ref=source, dst_ref=yb1.at[i, :, pl.ds(0, rows)],
            send_sem=y_s.at[0], recv_sem=l1_r.at[i], device_id=hop_to, device_id_type=MESH,
        )

    def hop2(i, rows=KB):
        return pltpu.make_async_remote_copy(
            src_ref=yb1.at[i, :, pl.ds(0, rows)], dst_ref=yb2.at[i, :, pl.ds(0, rows)],
            send_sem=y_s.at[0], recv_sem=l2_r.at[i], device_id=hop_to, device_id_type=MESH,
        )

    def turn(i):
        return pltpu.make_async_remote_copy(
            src_ref=yb2.at[i], dst_ref=yb3.at[i],
            send_sem=t_s.at[0], recv_sem=t_r.at[i], device_id=row_to, device_id_type=MESH,
        )

    def end(i, src, rows=KB):
        if i < LP - 1:
            target = u3a.at[pl.ds(SD, SD), pl.ds(i * KB, KB)]
        else:
            target = (u3b if i == LP - 1 else u2b).at[pl.ds(SD, SD), pl.ds(0, rows)]
        return pltpu.make_async_remote_copy(
            src_ref=src.at[i, :, pl.ds(0, rows)], dst_ref=target,
            send_sem=y_s.at[0], recv_sem=l3_r.at[max(0, i - LP + 2)], device_id=end_to, device_id_type=MESH,
        )

    H = W // 2

    def direct(b, k):
        return pltpu.make_async_remote_copy(
            src_ref=half.at[b, (xp, xm)[k]], dst_ref=hr.at[b, me],
            send_sem=x_s.at[0], recv_sem=x_r.at[b],
            device_id=(right, left)[k], device_id_type=MESH,
        )

    def relay1(b, k):
        return pltpu.make_async_remote_copy(
            src_ref=half.at[b, xo, pl.ds(k * H, H)], dst_ref=rbuf.at[b, k],
            send_sem=x_s.at[0], recv_sem=r1_r.at[b],
            device_id=(right, left)[k], device_id_type=MESH,
        )

    def relay2(b, k):
        return pltpu.make_async_remote_copy(
            src_ref=rbuf.at[b, k], dst_ref=hr.at[b, (xm, xp)[k], pl.ds(k * H, H)],
            send_sem=x_s.at[0], recv_sem=x_r.at[b],
            device_id=(right, left)[k], device_id_type=MESH,
        )

    def first_product(b, q, d):
        return lax.dot_general(
            uo[d, q], fer[b], (((0,), (0,)), ((), ())), preferred_element_type=jnp.float32
        ).astype(jnp.bfloat16)

    def one(condition):
        return jnp.where(condition, 1, 0)

    greeted = jnp.where(
        core == 1, 3 + one(head_peer), 5 - one(head) + one(turns & (z != 0)) + one(turn_peer)
    )
    pl.semaphore_wait(barrier, greeted - 2 * one(me == 0) - one((me == 1) | (me == NS - 1)))

    @pl.when((me == 1) | (me == NS // 2))
    def _():
        pl.semaphore_signal(x_answer, inc=1, device_id=left, device_id_type=MESH)

    @pl.when(me >= NS // 2)
    def _():
        pl.semaphore_signal(x_answer, inc=1, device_id=right, device_id_type=MESH)

    @pl.when(turn_peer)
    def _():
        pl.semaphore_signal(answer, inc=1, device_id=row_from, device_id_type=MESH)

    @pl.when(head_peer)
    def _():
        pl.semaphore_signal(answer, inc=1, device_id=after, device_id_type=MESH)

    def send_chunks():
        for copy in (follow0, follow1, follow2a):
            copy.start()

    @pl.when((core == 0) & jnp.logical_not(head))
    def _():
        send_chunks()
        follow2b.start()

    @pl.when(spare)
    def _():
        follow3c.start()

    @pl.when(core == 0)
    def _():
        for i in range(LP - 1):
            hop1(i).start()

    @pl.when((core == 0) & jnp.logical_not(spare))
    def _():
        hop1(LP - 1).start()

    @pl.when(spare)
    def _():
        hop1(LP - 1, KH).start()

    @pl.when(head)
    def _():
        hop1(LP).start()

    load_f(0, 0, 0).wait()
    load_uo(xo, 0).wait()
    for j in (xm, me):
        load_uo(j, 0).start()
    for k in range(2):
        half[0, xo, k * H:(k + 1) * H] = lax.dot_general(
            uo[xo, 0, :, k * H:(k + 1) * H], fer[0], (((0,), (0,)), ((), ())),
            preferred_element_type=jnp.float32,
        ).astype(jnp.bfloat16)

    @pl.when(me == 0)
    def _():
        pl.semaphore_wait(x_answer, 2)

    @pl.when((me == 1) | (me == NS - 1))
    def _():
        pl.semaphore_wait(x_answer, 1)

    relay1(0, 0).start()
    for f in range(1, FL):
        load_f(f, f, 0).start()
    for j in range(NS):
        load_uo(j, 1).start()
    for f in range(FL):
        load_f(FL + f, f, 1).start()
    load_uo(xp, 0).wait()
    half[0, xp] = first_product(0, 0, xp)
    relay1(0, 1).start()
    load_uo(xm, 0).wait()
    half[0, xm] = first_product(0, 0, xm)
    direct(0, 0).start()
    load_uo(me, 0).wait()
    hr[0, me] = first_product(0, 0, me)
    direct(0, 1).start()
    second = uo.at[:, 1]
    pltpu.make_async_copy(second, second, lu.at[NS]).wait()

    def stage1(b, _):
        q = b // FL
        load_f(b, 0, 0).wait()
        half[b, xo] = first_product(b, q, xo)
        half[b, xp] = first_product(b, q, xp)
        relay1(b, 0).start()
        relay1(b, 1).start()
        half[b, xm] = first_product(b, q, xm)
        direct(b, 0).start()
        hr[b, me] = first_product(b, q, me)
        direct(b, 1).start()
        return 0

    lax.fori_loop(1, 2, stage1, 0)

    @pl.when(head)
    def _():
        pl.semaphore_wait(answer, 1)
        send_chunks()

    lax.fori_loop(2, B, stage1, 0)
    for copy in own_u():
        copy.start()

    @pl.when(core == 1)
    def _():
        for copy in (follow0, follow1, follow2a, follow2b, follow3a, follow3b):
            copy.start()

    def forward_x(b):
        pltpu.make_async_copy(rbuf.at[b], rbuf.at[b], r1_r.at[b]).wait()
        for k in range(2):
            relay2(b, k).start()

    def forward_y1(i):
        short = (i == LP - 1) & head
        if i < LP:
            @pl.when((core == 0) & jnp.logical_not(short))
            def _():
                hop1(i).wait_recv()
                hop2(i).start()

        if i >= LP - 1:
            rows = KH if i == LP - 1 else KB

            @pl.when(short if i == LP - 1 else passes)
            def _():
                hop1(i, rows).wait_recv()
                hop2(i, rows).start()

    def forward_y2(i):
        short = (i == LP - 1) & passes
        if i < LP:
            @pl.when((core == 0) & jnp.logical_not(turns | short))
            def _():
                hop2(i).wait_recv()
                end(i, yb2).start()

        @pl.when((core == 0) & turns if i < LP else turn_head)
        def _():
            hop2(i).wait_recv()
            if i == 0:
                @pl.when(turn_head)
                def _():
                    pl.semaphore_wait(answer, 1)

            turn(i).start()

        if i == LP - 1:
            @pl.when(passes)
            def _():
                hop2(i, KH).wait_recv()
                end(i, yb2, KH).start()

    def forward_end(i):
        @pl.when((core == 0) & turns if i < LP else turn_peer)
        def _():
            turn(i).wait_recv()
            end(i, yb3).start()

    forward_y1(0)
    forward_x(0)
    forward_y1(1)
    forward_x(1)
    forward_y1(2)
    forward_y1(3)
    forward_x(2)
    forward_y2(0)
    forward_y1(4)
    forward_x(3)
    forward_y2(1)
    forward_end(0)
    forward_y2(2)
    forward_x(4)
    forward_end(1)
    forward_y2(3)
    forward_end(2)
    forward_x(5)
    forward_y2(4)
    forward_end(3)
    forward_end(4)

    load_partner.wait()
    pltpu.make_async_copy(uo, uo, lo.at[0]).wait()

    def locate(b):
        q = b // FL
        f = b - q * FL
        return f, q, lax.rem(partner[q, f] - first_sector + SECS * SD, 2 * SD)

    def rows_of(b, low, high):
        return jnp.concatenate([hr[b, s] for s in range(low, high)], axis=1)

    def times(rows, ref, index):
        return jnp.dot(rows, ref[index], preferred_element_type=jnp.float32)

    def arrive(b):
        here = hr.at[b, pl.ds(0, NS - 1)]
        pltpu.make_async_copy(here, here, x_r.at[b]).wait()

    def whole(b):
        f, q, index = locate(b)
        rows = rows_of(b, 0, NS)
        out[f, q, :, 0:W] = times(rows, u0, index).astype(jnp.bfloat16)
        out[f, q, :, W:2 * W] = times(rows, u1, index).astype(jnp.bfloat16)

    def part(b, j):
        f, q, index = locate(b)
        acc[b, j] = times(rows_of(b, 0, NS - 1), (u2a, u3a)[j], index)

    def rest(b, j):
        f, q, index = locate(b)
        value = acc[b, j] + times(hr[b, NS - 1], (u2b, u3b)[j], index)
        out[f, q, :, (2 + j) * W:(3 + j) * W] = value.astype(jnp.bfloat16)

    def early(b, _):
        arrive(b)
        whole(b)
        return 0

    def late(b, _):
        arrive(b)
        whole(b)
        part(b, 0)
        part(b, 1)
        return 0

    def complete(b, _):
        arrive(b)
        whole(b)
        f, q, index = locate(b)
        most, rows = rows_of(b, 0, NS - 1), hr[b, NS - 1]
        for j, (ua, ub) in enumerate(((u2a, u2b), (u3a, u3b))):
            value = times(most, ua, index) + times(rows, ub, index)
            out[f, q, :, (2 + j) * W:(3 + j) * W] = value.astype(jnp.bfloat16)
        return 0

    def parts(j, low, high):
        def body(b, _):
            part(b, j)
            return 0

        lax.fori_loop(low, high, body, 0, unroll=True)

    def last(j):
        def body(b, _):
            rest(b, j)
            return 0

        lax.fori_loop(0, B, body, 0, unroll=True)

    def long_way():
        pieces = u3a.at[pl.ds(SD, SD)]
        pltpu.make_async_copy(pieces, pieces, l3_r.at[0]).wait()

    @pl.when(core == 0)
    def _():
        for copy in (follow0, follow1, follow2a, follow2b, follow3a, follow3b):
            copy.wait_recv()
        lax.fori_loop(0, B, complete, 0)

    late_direct = head_peer | ((core == 1) & (y == NY - 1) & (z == nz // 2 - 1))

    @pl.when(core == 1)
    def _():
        follow0.wait_recv()
        follow1.wait_recv()
        lax.fori_loop(0, B - 2, early, 0)

        @pl.when(late_direct)
        def _():
            early(B - 2, 0)
            long_way()
            parts(1, 0, B - 1)
            follow2a.wait_recv()
            parts(0, 0, B - 1)
            late(B - 1, 0)

        @pl.when(jnp.logical_not(late_direct))
        def _():
            follow2a.wait_recv()
            parts(0, 0, B - 2)
            early(B - 2, 0)
            part(B - 2, 0)
            long_way()
            parts(1, 0, B - 1)
            late(B - 1, 0)
            follow2b.wait_recv()
            last(0)

        @pl.when(jnp.logical_not(spare_to))
        def _():
            end(LP - 1, yb2).wait_recv()

        @pl.when(spare_to)
        def _():
            end(LP - 1, yb2, KH).wait_recv()
            follow3c.wait_recv()

        last(1)

        @pl.when(late_direct)
        def _():
            @pl.when(head_peer)
            def _():
                end(LP, yb2).wait_recv()

            @pl.when(jnp.logical_not(head_peer))
            def _():
                follow2b.wait_recv()

            last(0)

    def sent(ref, sem):
        pltpu.make_async_copy(ref, ref, sem.at[0]).wait()

    sent(hr, x_s)

    @pl.when(core == 0)
    def _():
        sent(fer, y_s)
        sent(half.at[pl.ds(0, B - 1)], y_s)

        @pl.when(jnp.logical_not(head))
        def _():
            sent(half.at[0], y_s)

        @pl.when(head)
        def _():
            sent(half.at[0, pl.ds(0, 3)], y_s)

        @pl.when(passes)
        def _():
            sent(half.at[0, 0], y_s)

        @pl.when(turn_peer)
        def _():
            sent(half.at[0, pl.ds(0, 2)], y_s)

        @pl.when(turns)
        def _():
            sent(yb2.at[pl.ds(0, LP)], t_s)

        @pl.when(turn_head)
        def _():
            sent(yb2.at[LP], t_s)

    @pl.when(core == 1)
    def _():
        sent(uo, y_s)


def local(basis, fermion, partner):
    bf16 = jnp.bfloat16
    dma = pltpu.SemaphoreType.DMA
    result = pl.pallas_call(
        kernel,
        out_shape=pltpu.VMEM((FL, SD, W, NB), bf16),
        in_specs=[
            pl.BlockSpec(memory_space=pltpu.HBM),
            pl.BlockSpec(memory_space=pltpu.HBM),
            pl.BlockSpec(memory_space=pltpu.HBM),
        ],
        out_specs=pl.BlockSpec(memory_space=pltpu.VMEM),
        scratch_shapes=[
            pltpu.VMEM((NS, SD, NB, W), bf16),
            pltpu.VMEM((2 * SD, NB, W), bf16),
            pltpu.VMEM((2 * SD, NB, W), bf16),
            pltpu.VMEM((2 * SD, KA, W), bf16),
            pltpu.VMEM((2 * SD, KB, W), bf16),
            pltpu.VMEM((2 * SD, KA, W), bf16),
            pltpu.VMEM((2 * SD, KB, W), bf16),
            pltpu.VMEM((B, NB, W), bf16),
            pltpu.VMEM((B, NS, W, W), bf16),
            pltpu.VMEM((B, NS, W, W), bf16),
            pltpu.VMEM((B, 2, W // 2, W), bf16),
            pltpu.VMEM((LP + 1, SD, KB, W), bf16),
            pltpu.VMEM((LP + 1, SD, KB, W), bf16),
            pltpu.VMEM((LP + 1, SD, KB, W), bf16),
            pltpu.VMEM((B, 2, W, W), jnp.float32),
            dma((NS + 1,)), dma((B,)), dma((1,)),
            dma((1,)), dma((B,)), dma((B,)),
            dma((1,)), dma((6,)), dma((LP + 1,)), dma((LP + 1,)), dma((3,)), dma((1,)), dma((LP + 1,)), pltpu.SemaphoreType.REGULAR, pltpu.SemaphoreType.REGULAR,
            pltpu.SMEM((SD, FL), jnp.int32), dma((1,)),
        ],
        compiler_params=pltpu.CompilerParams(
            collective_id=0, has_side_effects=True, vmem_limit_bytes=56 * 2**20
        ),
    )(basis, fermion, partner.T)
    return result


def solution(mesh):
    placed = (P("sec", None, None), P(None, "sec", None, "slab"), P(None, "sec"))
    return jax.shard_map(
        local, mesh=mesh, in_specs=placed, out_specs=P(None, "sec", "slab", None), check_vma=False
    )
```

```python
import functools

import jax
import jax.numpy as jnp
from jax import lax
from jax.experimental import pallas as pl
from jax.experimental.pallas import tpu as pltpu
from jax.sharding import PartitionSpec as P

MESH = pl.DeviceIdType.MESH
NB = 1024
W = 256
NS = 4
FL = 3
SD = 2
B = FL * SD
SECS = 64
NY = 4
LP = 4
KB = NB // LP
KA = NB - KB
KH = KB // 2


def kernel(
    basis, fermion, partner_in, out,
    uo, u0, u1, u2a, u2b, u3a, u3b, fer, half, hr, rbuf, yb1, yb2, yb3, acc,
    lu, lf, lo, sent_s, x_r, r1_r, y_r, l1_r, l2_r, l3_r, t_r, answer, x_answer, partner, p_s,
):
    sec = lax.axis_index("sec")
    me = lax.axis_index("slab")
    core = lax.rem(sec, 2)
    chip = sec // 2
    y = lax.rem(chip, NY)
    z = chip // NY
    nz = SECS // (2 * NY)
    xp, xm = lax.rem(me + 1, NS), lax.rem(me + 3, NS)
    xo = lax.rem(me + 2, NS)
    right, left = (sec, xp), (sec, xm)
    before = (lax.rem(sec + SECS - 1, SECS), me)
    after = (lax.rem(sec + 1, SECS), me)
    y_up, y_dn = lax.rem(y + 1, NY), lax.rem(y + NY - 1, NY)
    hop_to = ((z * NY + y_up) * 2, me)
    hop_from = ((z * NY + y_dn) * 2, me)
    row_dn, row_up = lax.rem(z + nz - 1, nz), lax.rem(z + 1, nz)
    row_to = ((row_dn * NY + y) * 2, me)
    row_from = ((row_up * NY + y) * 2, me)
    end_to = ((z * NY + y_up) * 2 + 1, me)
    end_from = ((z * NY + y_dn) * 2, me)
    turns = y == 2
    first_sector = sec * SD

    head = (core == 0) & (y == 0) & (z == 0)
    head_peer = (core == 1) & (y == NY - 1) & (z == nz - 1)
    turn_head = (core == 0) & turns & (z == 0)
    turn_peer = (core == 0) & turns & (z == nz - 1)
    passes = (core == 0) & (y == 1) & (z == 0)
    spare = (core == 0) & (y == 3) & (z == 0)
    spare_to = (core == 1) & (y == 2) & (z == 0)
    barrier = pltpu.get_barrier_semaphore()

    def greet(device):
        pl.semaphore_signal(barrier, inc=1, device_id=device, device_id_type=MESH)

    @pl.when(me < NS // 2)
    def _():
        greet(right)

    @pl.when((me == 0) | (me == NS - 1))
    def _():
        greet(left)

    @pl.when(jnp.logical_not(head_peer))
    def _():
        greet(after)

    @pl.when(core == 0)
    def _():
        greet(hop_from)

    @pl.when(core == 1)
    def _():
        greet(end_from)

    @pl.when((core == 0) & turns & (z != nz - 1))
    def _():
        greet(row_from)

    @pl.when(head)
    def _():
        greet(before)

    @pl.when(turn_head)
    def _():
        greet(row_to)

    def load_uo(j, q):
        return pltpu.make_async_copy(
            basis.at[q, :, pl.ds(pl.multiple_of(j * W, W), W)], uo.at[j, q], lu.at[j if q == 0 else NS]
        )

    def load_f(b, f, q):
        return pltpu.make_async_copy(fermion.at[f, q], fer.at[b], lf.at[min(b, 1)])

    def load_u(ref, j, row, rows):
        return pltpu.make_async_copy(
            basis.at[:, pl.ds(row, rows), pl.ds(j * W, W)], ref.at[pl.ds(0, SD)], lo.at[0]
        )

    def own_u():
        places = ((u0, 0, 0, NB), (u1, 1, 0, NB), (u2a, 2, 0, KA), (u2b, 2, KA, KB),
                  (u3a, 3, 0, KA), (u3b, 3, KA, KB))
        return [load_u(*place) for place in places]

    load_partner = pltpu.make_async_copy(partner_in, partner, p_s.at[0])
    load_f(0, 0, 0).start()
    load_uo(xo, 0).start()
    load_uo(xp, 0).start()
    load_partner.start()

    def follow(src, dst, n):
        return pltpu.make_async_remote_copy(
            src_ref=src, dst_ref=dst.at[pl.ds(SD, SD)],
            send_sem=sent_s.at[0], recv_sem=y_r.at[n], device_id=before, device_id_type=MESH,
        )

    follow0 = follow(basis.at[:, :, pl.ds(0, W)], u0, 0)
    follow1 = follow(basis.at[:, :, pl.ds(W, W)], u1, 0)
    follow2a = follow(basis.at[:, pl.ds(0, KA), pl.ds(2 * W, W)], u2a, 2)
    follow2b = follow(basis.at[:, pl.ds(KA, KB), pl.ds(2 * W, W)], u2b, 3)
    follow3a = follow(basis.at[:, pl.ds(0, KA), pl.ds(3 * W, W)], u3a, 4)
    follow3b = follow(basis.at[:, pl.ds(KA, KB), pl.ds(3 * W, W)], u3b, 5)

    follow3c = pltpu.make_async_remote_copy(
        src_ref=basis.at[:, pl.ds(KA + KH, KH), pl.ds(3 * W, W)],
        dst_ref=u3b.at[pl.ds(SD, SD), pl.ds(KH, KH)],
        send_sem=sent_s.at[0], recv_sem=y_r.at[5], device_id=before, device_id_type=MESH,
    )

    def hop1(i, rows=KB):
        if i < LP:
            source = basis.at[:, pl.ds(i * KB, rows), pl.ds(3 * W, W)]
        else:
            source = basis.at[:, pl.ds(KA, KB), pl.ds(2 * W, W)]
        return pltpu.make_async_remote_copy(
            src_ref=source, dst_ref=yb1.at[i, :, pl.ds(0, rows)],
            send_sem=sent_s.at[0], recv_sem=l1_r.at[i], device_id=hop_to, device_id_type=MESH,
        )

    def hop2(i, rows=KB):
        return pltpu.make_async_remote_copy(
            src_ref=yb1.at[i, :, pl.ds(0, rows)], dst_ref=yb2.at[i, :, pl.ds(0, rows)],
            send_sem=sent_s.at[0], recv_sem=l2_r.at[i], device_id=hop_to, device_id_type=MESH,
        )

    def turn(i):
        return pltpu.make_async_remote_copy(
            src_ref=yb2.at[i], dst_ref=yb3.at[i],
            send_sem=sent_s.at[0], recv_sem=t_r.at[i], device_id=row_to, device_id_type=MESH,
        )

    def end(i, src, rows=KB):
        if i < LP - 1:
            target = u3a.at[pl.ds(SD, SD), pl.ds(i * KB, KB)]
        else:
            target = (u3b if i == LP - 1 else u2b).at[pl.ds(SD, SD), pl.ds(0, rows)]
        return pltpu.make_async_remote_copy(
            src_ref=src.at[i, :, pl.ds(0, rows)], dst_ref=target,
            send_sem=sent_s.at[0], recv_sem=l3_r.at[max(0, i - LP + 2)], device_id=end_to, device_id_type=MESH,
        )

    H = W // 2

    def direct(b, k):
        return pltpu.make_async_remote_copy(
            src_ref=half.at[b, (xp, xm)[k]], dst_ref=hr.at[b, me],
            send_sem=sent_s.at[0], recv_sem=x_r.at[b],
            device_id=(right, left)[k], device_id_type=MESH,
        )

    def relay1(b, k):
        return pltpu.make_async_remote_copy(
            src_ref=half.at[b, xo, pl.ds(k * H, H)], dst_ref=rbuf.at[b, k],
            send_sem=sent_s.at[0], recv_sem=r1_r.at[b],
            device_id=(right, left)[k], device_id_type=MESH,
        )

    def relay2(b, k):
        return pltpu.make_async_remote_copy(
            src_ref=rbuf.at[b, k], dst_ref=hr.at[b, (xm, xp)[k], pl.ds(k * H, H)],
            send_sem=sent_s.at[0], recv_sem=x_r.at[b],
            device_id=(right, left)[k], device_id_type=MESH,
        )

    def first_product(b, q, d):
        return lax.dot_general(
            uo[d, q], fer[b], (((0,), (0,)), ((), ())), preferred_element_type=jnp.float32
        ).astype(jnp.bfloat16)

    def one(condition):
        return jnp.where(condition, 1, 0)

    greeted = jnp.where(
        core == 1, 3 + one(head_peer), 5 - one(head) + one(turns & (z != 0)) + one(turn_peer)
    )
    pl.semaphore_wait(barrier, greeted - 2 * one(me == 0) - one((me == 1) | (me == NS - 1)))

    @pl.when((me == 1) | (me == NS // 2))
    def _():
        pl.semaphore_signal(x_answer, inc=1, device_id=left, device_id_type=MESH)

    @pl.when(me >= NS // 2)
    def _():
        pl.semaphore_signal(x_answer, inc=1, device_id=right, device_id_type=MESH)

    @pl.when(turn_peer)
    def _():
        pl.semaphore_signal(answer, inc=1, device_id=row_from, device_id_type=MESH)

    @pl.when(head_peer)
    def _():
        pl.semaphore_signal(answer, inc=1, device_id=after, device_id_type=MESH)

    def send_chunks():
        for copy in (follow0, follow1, follow2a):
            copy.start()

    @pl.when((core == 0) & jnp.logical_not(head))
    def _():
        send_chunks()
        follow2b.start()

    @pl.when(spare)
    def _():
        follow3c.start()

    @pl.when(core == 0)
    def _():
        for i in range(LP - 1):
            hop1(i).start()

    @pl.when((core == 0) & jnp.logical_not(spare))
    def _():
        hop1(LP - 1).start()

    @pl.when(spare)
    def _():
        hop1(LP - 1, KH).start()

    @pl.when(head)
    def _():
        hop1(LP).start()

    load_f(0, 0, 0).wait()
    load_uo(xo, 0).wait()
    for j in (xm, me):
        load_uo(j, 0).start()
    for k in range(2):
        half[0, xo, k * H:(k + 1) * H] = lax.dot_general(
            uo[xo, 0, :, k * H:(k + 1) * H], fer[0], (((0,), (0,)), ((), ())),
            preferred_element_type=jnp.float32,
        ).astype(jnp.bfloat16)

    @pl.when(me == 0)
    def _():
        pl.semaphore_wait(x_answer, 2)

    @pl.when((me == 1) | (me == NS - 1))
    def _():
        pl.semaphore_wait(x_answer, 1)

    relay1(0, 0).start()
    for f in range(1, FL):
        load_f(f, f, 0).start()
    for j in range(NS):
        load_uo(j, 1).start()
    for f in range(FL):
        load_f(FL + f, f, 1).start()
    load_uo(xp, 0).wait()
    half[0, xp] = first_product(0, 0, xp)
    relay1(0, 1).start()
    load_uo(xm, 0).wait()
    half[0, xm] = first_product(0, 0, xm)
    direct(0, 0).start()
    load_uo(me, 0).wait()
    hr[0, me] = first_product(0, 0, me)
    direct(0, 1).start()
    second = uo.at[:, 1]
    pltpu.make_async_copy(second, second, lu.at[NS]).wait()

    others = fer.at[pl.ds(1, B - 1)]
    pltpu.make_async_copy(others, others, lf.at[1]).wait()

    def stage1(b, _):
        q = b // FL
        half[b, xo] = first_product(b, q, xo)
        half[b, xp] = first_product(b, q, xp)
        relay1(b, 0).start()
        relay1(b, 1).start()
        half[b, xm] = first_product(b, q, xm)
        direct(b, 0).start()
        hr[b, me] = first_product(b, q, me)
        direct(b, 1).start()
        return 0

    lax.fori_loop(1, 2, stage1, 0)

    @pl.when(head)
    def _():
        pl.semaphore_wait(answer, 1)
        send_chunks()

    lax.fori_loop(2, B, stage1, 0)
    for copy in own_u():
        copy.start()

    @pl.when(core == 1)
    def _():
        for copy in (follow0, follow1, follow2a, follow2b, follow3a, follow3b):
            copy.start()

    def forward_x(b):
        pltpu.make_async_copy(rbuf.at[b], rbuf.at[b], r1_r.at[b]).wait()
        for k in range(2):
            relay2(b, k).start()

    def forward_y1(i):
        short = (i == LP - 1) & head
        if i < LP:
            @pl.when((core == 0) & jnp.logical_not(short))
            def _():
                hop1(i).wait_recv()
                hop2(i).start()

        if i >= LP - 1:
            rows = KH if i == LP - 1 else KB

            @pl.when(short if i == LP - 1 else passes)
            def _():
                hop1(i, rows).wait_recv()
                hop2(i, rows).start()

    def forward_y2(i):
        short = (i == LP - 1) & passes
        if i < LP:
            @pl.when((core == 0) & jnp.logical_not(turns | short))
            def _():
                hop2(i).wait_recv()
                end(i, yb2).start()

        @pl.when((core == 0) & turns if i < LP else turn_head)
        def _():
            hop2(i).wait_recv()
            if i == 0:
                @pl.when(turn_head)
                def _():
                    pl.semaphore_wait(answer, 1)

            turn(i).start()

        if i == LP - 1:
            @pl.when(passes)
            def _():
                hop2(i, KH).wait_recv()
                end(i, yb2, KH).start()

    def forward_end(i):
        @pl.when((core == 0) & turns if i < LP else turn_peer)
        def _():
            turn(i).wait_recv()
            end(i, yb3).start()

    forward_y1(0)
    forward_x(0)
    forward_y1(1)
    forward_x(1)
    forward_y1(2)
    forward_y1(3)
    forward_x(2)
    forward_y2(0)
    forward_y1(4)
    forward_x(3)
    forward_y2(1)
    forward_end(0)
    forward_y2(2)
    forward_x(4)
    forward_end(1)
    forward_y2(3)
    forward_end(2)
    forward_x(5)
    forward_y2(4)
    forward_end(3)
    forward_end(4)

    load_partner.wait()
    pltpu.make_async_copy(uo, uo, lo.at[0]).wait()

    def locate(b):
        q = b // FL
        f = b - q * FL
        return f, q, lax.rem(partner[q, f] - first_sector + SECS * SD, 2 * SD)

    def rows_of(b, low, high):
        return jnp.concatenate([hr[b, s] for s in range(low, high)], axis=1)

    def times(rows, ref, index):
        return jnp.dot(rows, ref[index], preferred_element_type=jnp.float32)

    def arrive(b):
        here = hr.at[b, pl.ds(0, NS - 1)]
        pltpu.make_async_copy(here, here, x_r.at[b]).wait()

    def whole(b):
        f, q, index = locate(b)
        rows = rows_of(b, 0, NS)
        out[f, q, :, 0:W] = times(rows, u0, index).astype(jnp.bfloat16)
        out[f, q, :, W:2 * W] = times(rows, u1, index).astype(jnp.bfloat16)

    def part(b, j):
        f, q, index = locate(b)
        acc[b, j] = times(rows_of(b, 0, NS - 1), (u2a, u3a)[j], index)

    def rest(b, j):
        f, q, index = locate(b)
        value = acc[b, j] + times(hr[b, NS - 1], (u2b, u3b)[j], index)
        out[f, q, :, (2 + j) * W:(3 + j) * W] = value.astype(jnp.bfloat16)

    def early(b, _):
        arrive(b)
        whole(b)
        return 0

    def late(b, _):
        arrive(b)
        whole(b)
        part(b, 0)
        part(b, 1)
        return 0

    def complete(b, _):
        arrive(b)
        whole(b)
        f, q, index = locate(b)
        most, rows = rows_of(b, 0, NS - 1), hr[b, NS - 1]
        for j, (ua, ub) in enumerate(((u2a, u2b), (u3a, u3b))):
            value = times(most, ua, index) + times(rows, ub, index)
            out[f, q, :, (2 + j) * W:(3 + j) * W] = value.astype(jnp.bfloat16)
        return 0

    def parts(j, low, high):
        def body(b, _):
            part(b, j)
            return 0

        lax.fori_loop(low, high, body, 0, unroll=True)

    def last(j):
        def body(b, _):
            rest(b, j)
            return 0

        lax.fori_loop(0, B, body, 0, unroll=True)

    def long_way():
        pieces = u3a.at[pl.ds(SD, SD)]
        pltpu.make_async_copy(pieces, pieces, l3_r.at[0]).wait()

    def first_chunks():
        pltpu.make_async_copy(u0, u0, y_r.at[0]).wait()

    @pl.when(core == 0)
    def _():
        first_chunks()
        for copy in (follow2a, follow2b, follow3a, follow3b):
            copy.wait_recv()
        lax.fori_loop(0, B, complete, 0)

    late_direct = head_peer | ((core == 1) & (y == NY - 1) & (z == nz // 2 - 1))

    @pl.when(core == 1)
    def _():
        first_chunks()
        lax.fori_loop(0, B - 2, early, 0)

        @pl.when(late_direct)
        def _():
            early(B - 2, 0)
            long_way()
            parts(1, 0, B - 1)
            follow2a.wait_recv()
            parts(0, 0, B - 1)
            late(B - 1, 0)

        @pl.when(jnp.logical_not(late_direct))
        def _():
            follow2a.wait_recv()
            parts(0, 0, B - 2)
            early(B - 2, 0)
            part(B - 2, 0)
            long_way()
            parts(1, 0, B - 1)
            late(B - 1, 0)
            follow2b.wait_recv()
            last(0)

        @pl.when(jnp.logical_not(spare_to))
        def _():
            end(LP - 1, yb2).wait_recv()

        @pl.when(spare_to)
        def _():
            end(LP - 1, yb2, KH).wait_recv()
            follow3c.wait_recv()

        last(1)

        @pl.when(late_direct)
        def _():
            @pl.when(head_peer)
            def _():
                end(LP, yb2).wait_recv()

            @pl.when(jnp.logical_not(head_peer))
            def _():
                follow2b.wait_recv()

            last(0)

    def sent(ref):
        pltpu.make_async_copy(ref, ref, sent_s.at[0]).wait()

    sent(hr)

    @pl.when(core == 0)
    def _():
        sent(fer)
        sent(half.at[pl.ds(0, B - 1)])

        @pl.when(jnp.logical_not(head))
        def _():
            sent(half.at[0])

        @pl.when(head)
        def _():
            sent(half.at[0, pl.ds(0, 3)])

        @pl.when(passes)
        def _():
            sent(half.at[0, 0])

        @pl.when(turn_peer)
        def _():
            sent(half.at[0, pl.ds(0, 2)])

        @pl.when(turns)
        def _():
            sent(yb2.at[pl.ds(0, LP)])

        @pl.when(turn_head)
        def _():
            sent(yb2.at[LP])

    @pl.when(core == 1)
    def _():
        sent(uo)


def local(basis, fermion, partner):
    bf16 = jnp.bfloat16
    dma = pltpu.SemaphoreType.DMA
    result = pl.pallas_call(
        kernel,
        out_shape=pltpu.VMEM((FL, SD, W, NB), bf16),
        in_specs=[
            pl.BlockSpec(memory_space=pltpu.HBM),
            pl.BlockSpec(memory_space=pltpu.HBM),
            pl.BlockSpec(memory_space=pltpu.HBM),
        ],
        out_specs=pl.BlockSpec(memory_space=pltpu.VMEM),
        scratch_shapes=[
            pltpu.VMEM((NS, SD, NB, W), bf16),
            pltpu.VMEM((2 * SD, NB, W), bf16),
            pltpu.VMEM((2 * SD, NB, W), bf16),
            pltpu.VMEM((2 * SD, KA, W), bf16),
            pltpu.VMEM((2 * SD, KB, W), bf16),
            pltpu.VMEM((2 * SD, KA, W), bf16),
            pltpu.VMEM((2 * SD, KB, W), bf16),
            pltpu.VMEM((B, NB, W), bf16),
            pltpu.VMEM((B, NS, W, W), bf16),
            pltpu.VMEM((B, NS, W, W), bf16),
            pltpu.VMEM((B, 2, W // 2, W), bf16),
            pltpu.VMEM((LP + 1, SD, KB, W), bf16),
            pltpu.VMEM((LP + 1, SD, KB, W), bf16),
            pltpu.VMEM((LP + 1, SD, KB, W), bf16),
            pltpu.VMEM((B, 2, W, W), jnp.float32),
            dma((NS + 1,)), dma((2,)), dma((1,)),
            dma((1,)), dma((B,)), dma((B,)),
            dma((6,)), dma((LP + 1,)), dma((LP + 1,)), dma((3,)), dma((LP + 1,)),
            pltpu.SemaphoreType.REGULAR, pltpu.SemaphoreType.REGULAR,
            pltpu.SMEM((SD, FL), jnp.int32), dma((1,)),
        ],
        compiler_params=pltpu.CompilerParams(
            collective_id=0, has_side_effects=True, vmem_limit_bytes=56 * 2**20
        ),
    )(basis, fermion, partner.T)
    return result


def solution(mesh):
    placed = (P("sec", None, None), P(None, "sec", None, "slab"), P(None, "sec"))
    return jax.shard_map(
        local, mesh=mesh, in_specs=placed, out_specs=P(None, "sec", "slab", None), check_vma=False
    )
```

```python
import functools

import jax
import jax.numpy as jnp
from jax import lax
from jax.experimental import pallas as pl
from jax.experimental.pallas import tpu as pltpu
from jax.sharding import PartitionSpec as P

MESH = pl.DeviceIdType.MESH
NB = 1024
W = 256
NS = 4
FL = 3
SD = 2
B = FL * SD
SECS = 64
NY = 4
LP = 4
KB = NB // LP
KA = NB - KB
KH = KB // 2


def kernel(
    basis, fermion, partner_in, out,
    uo, u0, u1, u2a, u2b, u3a, u3b, fer, half, hr, rbuf, yb1, yb2, yb3, acc,
    lu, lf, lo, x_s, x_r, r1_r, y_s, y_r, l1_r, l2_r, l3_r, t_s, t_r, answer, x_answer, partner, p_s,
):
    sec = lax.axis_index("sec")
    me = lax.axis_index("slab")
    core = lax.rem(sec, 2)
    chip = sec // 2
    y = lax.rem(chip, NY)
    z = chip // NY
    nz = SECS // (2 * NY)
    xp, xm = lax.rem(me + 1, NS), lax.rem(me + 3, NS)
    xo = lax.rem(me + 2, NS)
    right, left = (sec, xp), (sec, xm)
    before = (lax.rem(sec + SECS - 1, SECS), me)
    after = (lax.rem(sec + 1, SECS), me)
    y_up, y_dn = lax.rem(y + 1, NY), lax.rem(y + NY - 1, NY)
    hop_to = ((z * NY + y_up) * 2, me)
    hop_from = ((z * NY + y_dn) * 2, me)
    row_dn, row_up = lax.rem(z + nz - 1, nz), lax.rem(z + 1, nz)
    row_to = ((row_dn * NY + y) * 2, me)
    row_from = ((row_up * NY + y) * 2, me)
    end_to = ((z * NY + y_up) * 2 + 1, me)
    end_from = ((z * NY + y_dn) * 2, me)
    turns = y == 2
    first_sector = sec * SD

    head = (core == 0) & (y == 0) & (z == 0)
    head_peer = (core == 1) & (y == NY - 1) & (z == nz - 1)
    turn_head = (core == 0) & turns & (z == 0)
    turn_peer = (core == 0) & turns & (z == nz - 1)
    passes = (core == 0) & (y == 1) & (z == 0)
    spare = (core == 0) & (y == 3) & (z == 0)
    spare_to = (core == 1) & (y == 2) & (z == 0)
    barrier = pltpu.get_barrier_semaphore()

    def greet(device):
        pl.semaphore_signal(barrier, inc=1, device_id=device, device_id_type=MESH)

    @pl.when(me < NS // 2)
    def _():
        greet(right)

    @pl.when((me == 0) | (me == NS - 1))
    def _():
        greet(left)

    @pl.when(jnp.logical_not(head_peer))
    def _():
        greet(after)

    @pl.when(core == 0)
    def _():
        greet(hop_from)

    @pl.when(core == 1)
    def _():
        greet(end_from)

    @pl.when((core == 0) & turns & (z != nz - 1))
    def _():
        greet(row_from)

    @pl.when(head)
    def _():
        greet(before)

    @pl.when(turn_head)
    def _():
        greet(row_to)

    def load_uo(j, q):
        return pltpu.make_async_copy(
            basis.at[q, :, pl.ds(pl.multiple_of(j * W, W), W)], uo.at[j, q], lu.at[j if q == 0 else NS]
        )

    def load_f(b, f, q):
        return pltpu.make_async_copy(fermion.at[f, q], fer.at[b], lf.at[b])

    def load_u(ref, j, row, rows):
        return pltpu.make_async_copy(
            basis.at[:, pl.ds(row, rows), pl.ds(j * W, W)], ref.at[pl.ds(0, SD)], lo.at[0]
        )

    def own_u():
        places = ((u0, 0, 0, NB), (u1, 1, 0, NB), (u2a, 2, 0, KA), (u2b, 2, KA, KB),
                  (u3a, 3, 0, KA), (u3b, 3, KA, KB))
        return [load_u(*place) for place in places]

    load_partner = pltpu.make_async_copy(partner_in, partner, p_s.at[0])
    load_f(0, 0, 0).start()
    load_uo(xo, 0).start()
    load_uo(xp, 0).start()
    load_partner.start()

    def follow(src, dst, n):
        return pltpu.make_async_remote_copy(
            src_ref=src, dst_ref=dst.at[pl.ds(SD, SD)],
            send_sem=y_s.at[0], recv_sem=y_r.at[n], device_id=before, device_id_type=MESH,
        )

    follow0 = follow(basis.at[:, :, pl.ds(0, W)], u0, 0)
    follow1 = follow(basis.at[:, :, pl.ds(W, W)], u1, 1)
    follow2a = follow(basis.at[:, pl.ds(0, KA), pl.ds(2 * W, W)], u2a, 2)
    follow2b = follow(basis.at[:, pl.ds(KA, KB), pl.ds(2 * W, W)], u2b, 3)
    follow3a = follow(basis.at[:, pl.ds(0, KA), pl.ds(3 * W, W)], u3a, 4)
    follow3b = follow(basis.at[:, pl.ds(KA, KB), pl.ds(3 * W, W)], u3b, 5)

    follow3c = pltpu.make_async_remote_copy(
        src_ref=basis.at[:, pl.ds(KA + KH, KH), pl.ds(3 * W, W)],
        dst_ref=u3b.at[pl.ds(SD, SD), pl.ds(KH, KH)],
        send_sem=y_s.at[0], recv_sem=y_r.at[5], device_id=before, device_id_type=MESH,
    )

    def hop1(i, rows=KB):
        if i < LP:
            source = basis.at[:, pl.ds(i * KB, rows), pl.ds(3 * W, W)]
        else:
            source = basis.at[:, pl.ds(KA, KB), pl.ds(2 * W, W)]
        return pltpu.make_async_remote_copy(
            src_ref=source, dst_ref=yb1.at[i, :, pl.ds(0, rows)],
            send_sem=y_s.at[0], recv_sem=l1_r.at[i], device_id=hop_to, device_id_type=MESH,
        )

    def hop2(i, rows=KB):
        return pltpu.make_async_remote_copy(
            src_ref=yb1.at[i, :, pl.ds(0, rows)], dst_ref=yb2.at[i, :, pl.ds(0, rows)],
            send_sem=y_s.at[0], recv_sem=l2_r.at[i], device_id=hop_to, device_id_type=MESH,
        )

    def turn(i):
        return pltpu.make_async_remote_copy(
            src_ref=yb2.at[i], dst_ref=yb3.at[i],
            send_sem=t_s.at[0], recv_sem=t_r.at[i], device_id=row_to, device_id_type=MESH,
        )

    def end(i, src, rows=KB):
        if i < LP - 1:
            target = u3a.at[pl.ds(SD, SD), pl.ds(i * KB, KB)]
        else:
            target = (u3b if i == LP - 1 else u2b).at[pl.ds(SD, SD), pl.ds(0, rows)]
        return pltpu.make_async_remote_copy(
            src_ref=src.at[i, :, pl.ds(0, rows)], dst_ref=target,
            send_sem=y_s.at[0], recv_sem=l3_r.at[max(0, i - LP + 2)], device_id=end_to, device_id_type=MESH,
        )

    H = W // 2

    def direct(b, k):
        return pltpu.make_async_remote_copy(
            src_ref=half.at[b, (xp, xm)[k]], dst_ref=hr.at[b, me],
            send_sem=x_s.at[0], recv_sem=x_r.at[b],
            device_id=(right, left)[k], device_id_type=MESH,
        )

    def relay1(b, k):
        return pltpu.make_async_remote_copy(
            src_ref=half.at[b, xo, pl.ds(k * H, H)], dst_ref=rbuf.at[b, k],
            send_sem=x_s.at[0], recv_sem=r1_r.at[b],
            device_id=(right, left)[k], device_id_type=MESH,
        )

    def relay2(b, k):
        return pltpu.make_async_remote_copy(
            src_ref=rbuf.at[b, k], dst_ref=hr.at[b, (xm, xp)[k], pl.ds(k * H, H)],
            send_sem=x_s.at[0], recv_sem=x_r.at[b],
            device_id=(right, left)[k], device_id_type=MESH,
        )

    def first_product(b, q, d):
        return lax.dot_general(
            uo[d, q], fer[b], (((0,), (0,)), ((), ())), preferred_element_type=jnp.float32
        ).astype(jnp.bfloat16)

    def one(condition):
        return jnp.where(condition, 1, 0)

    greeted = jnp.where(
        core == 1, 3 + one(head_peer), 5 - one(head) + one(turns & (z != 0)) + one(turn_peer)
    )
    pl.semaphore_wait(barrier, greeted - 2 * one(me == 0) - one((me == 1) | (me == NS - 1)))

    @pl.when((me == 1) | (me == NS // 2))
    def _():
        pl.semaphore_signal(x_answer, inc=1, device_id=left, device_id_type=MESH)

    @pl.when(me >= NS // 2)
    def _():
        pl.semaphore_signal(x_answer, inc=1, device_id=right, device_id_type=MESH)

    @pl.when(turn_peer)
    def _():
        pl.semaphore_signal(answer, inc=1, device_id=row_from, device_id_type=MESH)

    @pl.when(head_peer)
    def _():
        pl.semaphore_signal(answer, inc=1, device_id=after, device_id_type=MESH)

    def send_chunks():
        for copy in (follow0, follow1, follow2a):
            copy.start()

    @pl.when(core == 0)
    def _():
        for i in range(LP - 1):
            hop1(i).start()

    @pl.when((core == 0) & jnp.logical_not(spare))
    def _():
        hop1(LP - 1).start()

    @pl.when(spare)
    def _():
        hop1(LP - 1, KH).start()

    @pl.when(head)
    def _():
        hop1(LP).start()

    @pl.when((core == 0) & jnp.logical_not(head))
    def _():
        send_chunks()
        follow2b.start()

    @pl.when(spare)
    def _():
        follow3c.start()

    load_f(0, 0, 0).wait()
    load_uo(xo, 0).wait()
    for j in (xm, me):
        load_uo(j, 0).start()
    for k in range(2):
        half[0, xo, k * H:(k + 1) * H] = lax.dot_general(
            uo[xo, 0, :, k * H:(k + 1) * H], fer[0], (((0,), (0,)), ((), ())),
            preferred_element_type=jnp.float32,
        ).astype(jnp.bfloat16)

    @pl.when(me == 0)
    def _():
        pl.semaphore_wait(x_answer, 2)

    @pl.when((me == 1) | (me == NS - 1))
    def _():
        pl.semaphore_wait(x_answer, 1)

    relay1(0, 0).start()
    for f in range(1, FL):
        load_f(f, f, 0).start()
    for j in range(NS):
        load_uo(j, 1).start()
    for f in range(FL):
        load_f(FL + f, f, 1).start()
    load_uo(xp, 0).wait()
    half[0, xp] = first_product(0, 0, xp)
    relay1(0, 1).start()
    load_uo(xm, 0).wait()
    half[0, xm] = first_product(0, 0, xm)
    direct(0, 0).start()
    load_uo(me, 0).wait()
    hr[0, me] = first_product(0, 0, me)
    direct(0, 1).start()
    second = uo.at[:, 1]
    pltpu.make_async_copy(second, second, lu.at[NS]).wait()

    def stage1(b, _):
        q = b // FL
        load_f(b, 0, 0).wait()
        half[b, xo] = first_product(b, q, xo)
        half[b, xp] = first_product(b, q, xp)
        relay1(b, 0).start()
        relay1(b, 1).start()
        half[b, xm] = first_product(b, q, xm)
        direct(b, 0).start()
        hr[b, me] = first_product(b, q, me)
        direct(b, 1).start()
        return 0

    lax.fori_loop(1, 2, stage1, 0)

    @pl.when(head)
    def _():
        pl.semaphore_wait(answer, 1)
        send_chunks()

    lax.fori_loop(2, B, stage1, 0)
    for copy in own_u():
        copy.start()

    @pl.when(core == 1)
    def _():
        for copy in (follow0, follow1, follow2a, follow2b, follow3a, follow3b):
            copy.start()

    def forward_x(b):
        pltpu.make_async_copy(rbuf.at[b], rbuf.at[b], r1_r.at[b]).wait()
        for k in range(2):
            relay2(b, k).start()

    def forward_y1(i):
        short = (i == LP - 1) & head
        if i < LP:
            @pl.when((core == 0) & jnp.logical_not(short))
            def _():
                hop1(i).wait_recv()
                hop2(i).start()

        if i >= LP - 1:
            rows = KH if i == LP - 1 else KB

            @pl.when(short if i == LP - 1 else passes)
            def _():
                hop1(i, rows).wait_recv()
                hop2(i, rows).start()

    def forward_y2(i):
        short = (i == LP - 1) & passes
        if i < LP:
            @pl.when((core == 0) & jnp.logical_not(turns | short))
            def _():
                hop2(i).wait_recv()
                end(i, yb2).start()

        @pl.when((core == 0) & turns if i < LP else turn_head)
        def _():
            hop2(i).wait_recv()
            if i == 0:
                @pl.when(turn_head)
                def _():
                    pl.semaphore_wait(answer, 1)

            turn(i).start()

        if i == LP - 1:
            @pl.when(passes)
            def _():
                hop2(i, KH).wait_recv()
                end(i, yb2, KH).start()

    def forward_end(i):
        @pl.when((core == 0) & turns if i < LP else turn_peer)
        def _():
            turn(i).wait_recv()
            end(i, yb3).start()

    forward_y1(0)
    forward_x(0)
    forward_y1(1)
    forward_x(1)
    forward_y1(2)
    forward_y1(3)
    forward_x(2)
    forward_y2(0)
    forward_y1(4)
    forward_x(3)
    forward_y2(1)
    forward_end(0)
    forward_y2(2)
    forward_x(4)
    forward_end(1)
    forward_y2(3)
    forward_end(2)
    forward_x(5)
    forward_y2(4)
    forward_end(3)
    forward_end(4)

    load_partner.wait()
    pltpu.make_async_copy(uo, uo, lo.at[0]).wait()

    def locate(b):
        q = b // FL
        f = b - q * FL
        return f, q, lax.rem(partner[q, f] - first_sector + SECS * SD, 2 * SD)

    def rows_of(b, low, high):
        return jnp.concatenate([hr[b, s] for s in range(low, high)], axis=1)

    def times(rows, ref, index):
        return jnp.dot(rows, ref[index], preferred_element_type=jnp.float32)

    def arrive(b):
        here = hr.at[b, pl.ds(0, NS - 1)]
        pltpu.make_async_copy(here, here, x_r.at[b]).wait()

    def whole(b):
        f, q, index = locate(b)
        rows = rows_of(b, 0, NS)
        out[f, q, :, 0:W] = times(rows, u0, index).astype(jnp.bfloat16)
        out[f, q, :, W:2 * W] = times(rows, u1, index).astype(jnp.bfloat16)

    def part(b, j):
        f, q, index = locate(b)
        acc[b, j] = times(rows_of(b, 0, NS - 1), (u2a, u3a)[j], index)

    def rest(b, j):
        f, q, index = locate(b)
        value = acc[b, j] + times(hr[b, NS - 1], (u2b, u3b)[j], index)
        out[f, q, :, (2 + j) * W:(3 + j) * W] = value.astype(jnp.bfloat16)

    def early(b, _):
        arrive(b)
        whole(b)
        return 0

    def late(b, _):
        arrive(b)
        whole(b)
        part(b, 0)
        part(b, 1)
        return 0

    def complete(b, _):
        arrive(b)
        whole(b)
        f, q, index = locate(b)
        most, rows = rows_of(b, 0, NS - 1), hr[b, NS - 1]
        for j, (ua, ub) in enumerate(((u2a, u2b), (u3a, u3b))):
            value = times(most, ua, index) + times(rows, ub, index)
            out[f, q, :, (2 + j) * W:(3 + j) * W] = value.astype(jnp.bfloat16)
        return 0

    def parts(j, low, high):
        def body(b, _):
            part(b, j)
            return 0

        lax.fori_loop(low, high, body, 0, unroll=True)

    def last(j):
        def body(b, _):
            rest(b, j)
            return 0

        lax.fori_loop(0, B, body, 0, unroll=True)

    def long_way():
        pieces = u3a.at[pl.ds(SD, SD)]
        pltpu.make_async_copy(pieces, pieces, l3_r.at[0]).wait()

    @pl.when(core == 0)
    def _():
        for copy in (follow0, follow1, follow2a, follow2b, follow3a, follow3b):
            copy.wait_recv()
        lax.fori_loop(0, B, complete, 0)

    late_direct = head_peer | ((core == 1) & (y == NY - 1) & (z == nz // 2 - 1))

    @pl.when(core == 1)
    def _():
        follow0.wait_recv()
        follow1.wait_recv()
        lax.fori_loop(0, B - 2, early, 0)

        @pl.when(late_direct)
        def _():
            early(B - 2, 0)
            long_way()
            parts(1, 0, B - 1)
            follow2a.wait_recv()
            parts(0, 0, B - 1)
            late(B - 1, 0)

        @pl.when(jnp.logical_not(late_direct))
        def _():
            follow2a.wait_recv()
            parts(0, 0, B - 2)
            early(B - 2, 0)
            part(B - 2, 0)
            long_way()
            parts(1, 0, B - 1)
            late(B - 1, 0)
            follow2b.wait_recv()
            last(0)

        @pl.when(jnp.logical_not(spare_to))
        def _():
            end(LP - 1, yb2).wait_recv()

        @pl.when(spare_to)
        def _():
            end(LP - 1, yb2, KH).wait_recv()
            follow3c.wait_recv()

        last(1)

        @pl.when(late_direct)
        def _():
            @pl.when(head_peer)
            def _():
                end(LP, yb2).wait_recv()

            @pl.when(jnp.logical_not(head_peer))
            def _():
                follow2b.wait_recv()

            last(0)

    def sent(ref, sem):
        pltpu.make_async_copy(ref, ref, sem.at[0]).wait()

    sent(hr, x_s)

    @pl.when(core == 0)
    def _():
        sent(fer, y_s)
        sent(half.at[pl.ds(0, B - 1)], y_s)

        @pl.when(jnp.logical_not(head))
        def _():
            sent(half.at[0], y_s)

        @pl.when(head)
        def _():
            sent(half.at[0, pl.ds(0, 3)], y_s)

        @pl.when(passes)
        def _():
            sent(half.at[0, 0], y_s)

        @pl.when(turn_peer)
        def _():
            sent(half.at[0, pl.ds(0, 2)], y_s)

        @pl.when(turns)
        def _():
            sent(yb2.at[pl.ds(0, LP)], t_s)

        @pl.when(turn_head)
        def _():
            sent(yb2.at[LP], t_s)

    @pl.when(core == 1)
    def _():
        sent(uo, y_s)


def local(basis, fermion, partner):
    bf16 = jnp.bfloat16
    dma = pltpu.SemaphoreType.DMA
    result = pl.pallas_call(
        kernel,
        out_shape=pltpu.VMEM((FL, SD, W, NB), bf16),
        in_specs=[
            pl.BlockSpec(memory_space=pltpu.HBM),
            pl.BlockSpec(memory_space=pltpu.HBM),
            pl.BlockSpec(memory_space=pltpu.HBM),
        ],
        out_specs=pl.BlockSpec(memory_space=pltpu.VMEM),
        scratch_shapes=[
            pltpu.VMEM((NS, SD, NB, W), bf16),
            pltpu.VMEM((2 * SD, NB, W), bf16),
            pltpu.VMEM((2 * SD, NB, W), bf16),
            pltpu.VMEM((2 * SD, KA, W), bf16),
            pltpu.VMEM((2 * SD, KB, W), bf16),
            pltpu.VMEM((2 * SD, KA, W), bf16),
            pltpu.VMEM((2 * SD, KB, W), bf16),
            pltpu.VMEM((B, NB, W), bf16),
            pltpu.VMEM((B, NS, W, W), bf16),
            pltpu.VMEM((B, NS, W, W), bf16),
            pltpu.VMEM((B, 2, W // 2, W), bf16),
            pltpu.VMEM((LP + 1, SD, KB, W), bf16),
            pltpu.VMEM((LP + 1, SD, KB, W), bf16),
            pltpu.VMEM((LP + 1, SD, KB, W), bf16),
            pltpu.VMEM((B, 2, W, W), jnp.float32),
            dma((NS + 1,)), dma((B,)), dma((1,)),
            dma((1,)), dma((B,)), dma((B,)),
            dma((1,)), dma((6,)), dma((LP + 1,)), dma((LP + 1,)), dma((3,)), dma((1,)), dma((LP + 1,)), pltpu.SemaphoreType.REGULAR, pltpu.SemaphoreType.REGULAR,
            pltpu.SMEM((SD, FL), jnp.int32), dma((1,)),
        ],
        compiler_params=pltpu.CompilerParams(
            collective_id=0, has_side_effects=True, vmem_limit_bytes=56 * 2**20
        ),
    )(basis, fermion, partner.T)
    return result


def solution(mesh):
    placed = (P("sec", None, None), P(None, "sec", None, "slab"), P(None, "sec"))
    return jax.shard_map(
        local, mesh=mesh, in_specs=placed, out_specs=P(None, "sec", "slab", None), check_vma=False
    )
```
